512 devices in a mesh: req: 64 (over y, z), head: 8 (over x, core).
Axes of the slice: x: 4, y: 4, z: 16, core: 2. Of those that a mesh axis runs over, the one named last changes fastest.
Arguments:
- tokens: bfloat16 [256, 2048], P('req'), may hold values from -1.1953125 to 1.1953125
- lengths: int32 [256], replicated, may hold values from 1 to 1021, as said below
- kv_cache: bfloat16 [1, 2, 65536, 8, 128], P(None, None, 'req', 'head'), may hold values from -24 to 24
- w_qkv: bfloat16 [1, 2048, 8, 512], P(None, 'req', 'head'), may hold values from -0.125 to 0.125
- w_headgate: bfloat16 [1, 2048, 16], P(None, None, 'head'), may hold values from -0.125 to 0.125
- w_out: bfloat16 [1, 2048, 2048], P(None, 'head', 'req'), may hold values from -0.5 to 0.5
- in_gain: float32 [1, 2048], replicated, may hold values from 0.5 to 1.5
- q_gain: float32 [1, 128], replicated, may hold values from 0.1 to 1.9
- k_gain: float32 [1, 128], replicated, may hold values from 0.1 to 1.9
- post_gain: float32 [1, 2048], replicated, may hold values from 0.5 to 1.5
- w_gate: bfloat16 [1, 2048, 6144], P(None, 'head', 'req'), may hold values from -0.125 to 0.125
- w_up: bfloat16 [1, 2048, 6144], P(None, 'head', 'req'), may hold values from -0.125 to 0.125
- w_down: bfloat16 [1, 6144, 2048], P(None, 'req', 'head'), may hold values from -0.078125 to 0.078125
- final_gain: float32 [2048], replicated, may hold values from 0.5 to 1.5
- w_vocab: bfloat16 [2048, 131072], P(None, ('req', 'head')), may hold values from -0.125 to 0.125
Outputs:
- logits: bfloat16 [256, 131072], P(None, ('req', 'head'))
The draws below stay inside these ranges and needn't reach their ends.
Inputs may be any that keep to these rules, and one draw needn't show every extreme that they name: On every index of req the lengths of its 4 requests sum to at most 1024. On 8 indices, drawn anew, they sum to exactly 1024 and one request there is longer than 512; on one of these the other requests hold one token each. On every other index each length is at most 128 and one is exactly 128.
All inputs are finite; a program needn't handle non-finite values.
Results may differ from the reference program's by a relative error of at most 0.015.
Values may be sent and summed in bfloat16 or wider, within the bound.
No kernel may reach another device: no remote copies, remote signals or barrier semaphores. Data moves between devices by JAX's collectives and lax.ppermute only.
A program may use at most 64 MiB of HBM per device.

```python
import math
import jax
import jax.numpy as jnp
from jax import lax

D = 2048
HEADS = 16
KV_HEADS = 8
HD = 128
FF = 6144
VOCAB = 131072
LAYERS = 1
R_DEV = 4
SHORT = 128
REQS = 256
POOL = 1024
POOL_ALL = 65536
QKV_COLS = 512
LONG_DEVS = 8
N_REQ = 64


def draw_lengths(key, part):
    short_key = jax.random.fold_in(key, 11)
    chosen_key = jax.random.fold_in(key, 23)
    device_key = jax.random.fold_in(key, 37)
    device_count = REQS // R_DEV
    shorts = jax.random.randint(short_key, (device_count, R_DEV), 1, SHORT + 1)
    chosen_slot = jax.random.randint(chosen_key, (device_count,), 0, R_DEV)
    order = jax.random.permutation(device_key, device_count)
    long_flag = jnp.zeros((device_count,), jnp.int32).at[order[:LONG_DEVS]].set(1)
    extreme_flag = jnp.arange(device_count, dtype=jnp.int32) == order[0]
    shorts = jnp.where(extreme_flag[:, None], 1, shorts)
    chosen = jnp.arange(R_DEV, dtype=jnp.int32)[None, :] == chosen_slot[:, None]
    others = jnp.sum(jnp.where(chosen, 0, shorts), axis=1)
    long_length = POOL - others
    picked = jnp.where(long_flag == 1, long_length, SHORT)
    result = jnp.where(chosen, picked[:, None], shorts)
    return result.reshape(-1).astype(jnp.int32)


def draw_kv_cache(key, part):
    base_key = jax.random.fold_in(key, 101)
    place_key = jax.random.fold_in(key, 103)
    strength_key = jax.random.fold_in(key, 107)
    full_shape = (LAYERS, 2, POOL_ALL, KV_HEADS, HD)
    base = jax.random.truncated_normal(base_key, -3.0, 3.0, full_shape, jnp.float32)
    low_strength = 3.0
    high_strength = 8.0
    device_count = POOL_ALL // POOL
    spike_count = max(POOL // 256, 2)
    places = POOL // 2 + jax.random.randint(place_key, (LAYERS, device_count, spike_count), 0, POOL // 2)
    slot_index = jnp.arange(POOL, dtype=jnp.int32)
    struck = jnp.any(slot_index[None, None, :, None] == places[:, :, None, :], axis=-1)
    struck = struck.reshape(LAYERS, POOL_ALL)
    log_strength = jax.random.uniform(strength_key, (LAYERS, POOL_ALL, KV_HEADS), jnp.float32, math.log(low_strength), math.log(high_strength))
    key_factor = jnp.where(struck[:, :, None], jnp.exp(log_strength), 1.0)
    value_factor = jnp.where(struck[:, :, None], 2.0, 1.0) * jnp.ones((LAYERS, POOL_ALL, KV_HEADS), jnp.float32)
    factor = jnp.stack([key_factor, value_factor], axis=1)[..., None]
    return (base * factor).astype(jnp.bfloat16)


def block_levels(own_key, extent, shards, low, largest):
    def one(axis_at, blocks):
        draws = jax.random.uniform(jax.random.fold_in(jax.random.fold_in(own_key, 6), axis_at), (blocks,), jnp.float32, low / len(shards), largest / len(shards))
        return jnp.repeat(jnp.exp(draws), extent[axis_at] // blocks).reshape((-1,) + (1,) * (len(extent) - axis_at - 1))

    factor_of = one(*shards[0])
    for cut in shards[1:]:
        factor_of = factor_of * one(*cut)
    return factor_of


def normal_values(stream_key, dims, width, most, cuts=(), kind=jnp.bfloat16):
    values = jax.random.normal(stream_key, dims, jnp.float32) * width
    if len(cuts) > 0:
        values = block_levels(stream_key, dims, cuts, -0.22, 0.18) * values
    return jnp.clip(values, min=-most, max=most).astype(kind)


def setup_inputs(seed: int = 0) -> dict:
    keys = jax.random.split(jax.random.key(seed), 16)
    tokens = normal_values(keys[0], (REQS, D), 0.2, 1.1953125, ((0, 64),))
    lengths = draw_lengths(jax.random.fold_in(keys[15], 71), 0)
    kv_cache = draw_kv_cache(jax.random.fold_in(keys[15], 71), 0)
    w_qkv = normal_values(keys[3], (LAYERS, D, KV_HEADS, QKV_COLS), D ** -0.5, 0.125, ((1, 64), (2, 8)))
    w_headgate = normal_values(keys[4], (LAYERS, D, HEADS), D ** -0.5, 0.125, ((2, 8),))
    w_out = normal_values(keys[5], (LAYERS, HEADS * HD, D), HD ** -0.5, 0.5, ((1, 8), (2, 64)))
    in_gain = jnp.clip(1.0 + 0.1 * jax.random.normal(keys[6], (LAYERS, D), jnp.float32), 0.5, 1.5)
    q_gain = jnp.clip(1.0 + 0.18 * jax.random.normal(keys[7], (LAYERS, HD), jnp.float32), 0.1, 1.9)
    k_gain = jnp.clip(1.0 + 0.18 * jax.random.normal(keys[8], (LAYERS, HD), jnp.float32), 0.1, 1.9)
    post_gain = jnp.clip(1.0 + 0.1 * jax.random.normal(keys[9], (LAYERS, D), jnp.float32), 0.5, 1.5)
    w_gate = normal_values(keys[10], (LAYERS, D, FF), D ** -0.5, 0.125, ((1, 8), (2, 64)))
    w_up = normal_values(keys[11], (LAYERS, D, FF), D ** -0.5, 0.125, ((1, 8), (2, 64)))
    w_down = normal_values(keys[12], (LAYERS, FF, D), FF ** -0.5, 0.078125, ((1, 64), (2, 8)))
    final_gain = jnp.clip(1.0 + 0.1 * jax.random.normal(keys[13], (D,), jnp.float32), 0.5, 1.5)
    w_vocab = normal_values(keys[14], (D, VOCAB), D ** -0.5, 0.125, ((1, 512),))
    return {"tokens": tokens, "lengths": lengths, "kv_cache": kv_cache, "w_qkv": w_qkv, "w_headgate": w_headgate, "w_out": w_out, "in_gain": in_gain, "q_gain": q_gain, "k_gain": k_gain, "post_gain": post_gain, "w_gate": w_gate, "w_up": w_up, "w_down": w_down, "final_gain": final_gain, "w_vocab": w_vocab}


EPSILON = 1e-06
ROPE_THETA = 1000000.0

def rms_scale(values, gain):
    mean_square = lax.optimization_barrier(jnp.mean(values * values, axis=-1, keepdims=True))
    return values * lax.rsqrt(mean_square + EPSILON) * gain

def rotate(values, position):
    half_dim = values.shape[-1] // 2
    frequency = ROPE_THETA ** (-2.0 * jnp.arange(half_dim, dtype=jnp.float32) / values.shape[-1])
    angles = position.astype(jnp.float32)[:, None] * frequency[None, :]
    target_shape = (angles.shape[0],) + (1,) * (values.ndim - 2) + (half_dim,)
    cosine = jnp.cos(angles).reshape(target_shape)
    sine_part = jnp.sin(angles).reshape(target_shape)
    first_half = values[..., :half_dim]
    second = values[..., half_dim:]
    return jnp.concatenate([first_half * cosine - second * sine_part, second * cosine + first_half * sine_part], axis=-1)

def attend_device(queries, new_key, new_value, key_rows, value_rows, length_rows):
    score_scale = queries.shape[-1] ** (-0.5)
    starts = (jnp.cumsum(length_rows) - length_rows).astype(jnp.int32)
    limits = (starts + length_rows).astype(jnp.int32)
    slot_index = jnp.arange(key_rows.shape[0], dtype=jnp.int32)
    inside = (slot_index[None, :] >= starts[:, None]) & (slot_index[None, :] < limits[:, None])
    scores = jnp.einsum('rgqd,sgd->rgqs', queries.astype(jnp.float32), key_rows.astype(jnp.float32)) * score_scale
    weights = jnp.where(inside[:, None, None, :], jnp.exp(scores), 0.0)
    own_score = jnp.einsum('rgqd,rgd->rgq', queries.astype(jnp.float32), new_key.astype(jnp.float32)) * score_scale
    own_weight = jnp.exp(own_score)
    denominator = lax.optimization_barrier(jnp.sum(weights, axis=-1)) + own_weight
    rounded = lax.optimization_barrier(weights.astype(jnp.bfloat16)).astype(jnp.float32)
    own_rounded = lax.optimization_barrier(own_weight.astype(jnp.bfloat16)).astype(jnp.float32)
    summed = jnp.einsum('rgqs,sgd->rgqd', rounded, value_rows.astype(jnp.float32))
    summed = summed + own_rounded[..., None] * new_value.astype(jnp.float32)[:, :, None, :]
    return summed / denominator[..., None]

def reference(tokens, lengths, kv_cache, w_qkv, w_headgate, w_out, in_gain, q_gain, k_gain, post_gain, w_gate, w_up, w_down, final_gain, w_vocab):
    group_size = HEADS // KV_HEADS
    stream = tokens
    for layer_index in range(LAYERS):
        normed = rms_scale(stream.astype(jnp.float32), in_gain[layer_index]).astype(jnp.bfloat16)
        qkv = jnp.dot(normed, w_qkv[layer_index].reshape(D, KV_HEADS * QKV_COLS), preferred_element_type=jnp.float32)
        qkv = qkv.reshape(REQS, KV_HEADS, QKV_COLS)
        queries = qkv[:, :, :group_size * HD].reshape(REQS, KV_HEADS, group_size, HD)
        new_key = qkv[:, :, group_size * HD:(group_size + 1) * HD]
        new_value = qkv[:, :, (group_size + 1) * HD:].astype(jnp.bfloat16)
        queries = rotate(rms_scale(queries, q_gain[layer_index]), lengths).astype(jnp.bfloat16)
        new_key = rotate(rms_scale(new_key, k_gain[layer_index]), lengths).astype(jnp.bfloat16)
        head_gate = jax.nn.sigmoid(jnp.dot(normed, w_headgate[layer_index], preferred_element_type=jnp.float32))
        head_gate = head_gate.reshape(REQS, KV_HEADS, group_size)
        key_all = kv_cache[layer_index, 0]
        value_all = kv_cache[layer_index, 1]

        def one_device(device_index):
            first_row = (device_index * R_DEV).astype(jnp.int32)
            first_slot = (device_index * POOL).astype(jnp.int32)

            def request_rows(array):
                return lax.dynamic_slice_in_dim(array, first_row, R_DEV, 0)
            return attend_device(request_rows(queries), request_rows(new_key), request_rows(new_value), lax.dynamic_slice_in_dim(key_all, first_slot, POOL, 0), lax.dynamic_slice_in_dim(value_all, first_slot, POOL, 0), request_rows(lengths))
        attended = lax.map(one_device, jnp.arange(N_REQ, dtype=jnp.int32))
        attended = attended.reshape(REQS, KV_HEADS, group_size, HD)
        mixed_heads = (attended * head_gate[..., None]).astype(jnp.bfloat16).reshape(REQS, HEADS * HD)
        projected = jnp.dot(mixed_heads, w_out[layer_index], preferred_element_type=jnp.float32)
        stream = (stream.astype(jnp.float32) + projected).astype(jnp.bfloat16)
        normed_two = rms_scale(stream.astype(jnp.float32), post_gain[layer_index]).astype(jnp.bfloat16)
        gate_part = jnp.dot(normed_two, w_gate[layer_index], preferred_element_type=jnp.float32)
        up_part = jnp.dot(normed_two, w_up[layer_index], preferred_element_type=jnp.float32)
        hidden = (jax.nn.silu(gate_part) * up_part).astype(jnp.bfloat16)
        down_part = jnp.dot(hidden, w_down[layer_index], preferred_element_type=jnp.float32)
        stream = (stream.astype(jnp.float32) + down_part).astype(jnp.bfloat16)
    final_norm = rms_scale(stream.astype(jnp.float32), final_gain).astype(jnp.bfloat16)
    return jnp.dot(final_norm, w_vocab, preferred_element_type=jnp.float32).astype(jnp.bfloat16)
```

```python
import jax
import jax.numpy as jnp
from jax import lax
from jax.sharding import Mesh
from jax.sharding import PartitionSpec as P

EPSILON = 1e-06
ROPE_THETA = 1000000.0
Y, Z, X, C = 4, 16, 4, 2
F32, BF16 = jnp.float32, jnp.bfloat16


def rms_scale(values, gain):
    mean_square = jnp.mean(values * values, axis=-1, keepdims=True)
    return values * lax.rsqrt(mean_square + EPSILON) * gain


def rotate(values, cosine, sine):
    half = values.shape[-1] // 2
    a, b = values[..., :half], values[..., half:]
    return jnp.concatenate([a * cosine - b * sine, b * cosine + a * sine], axis=-1)


def swap(values, axes):
    return lax.all_to_all(values, axes, split_axis=0, concat_axis=0, tiled=True)


def spread(values, axes, count):
    return swap(jnp.broadcast_to(values[None], (count,) + values.shape), axes)


def local(
    tokens,
    lengths,
    kv_cache,
    w_qkv,
    w_headgate,
    w_out,
    in_gain,
    q_gain,
    k_gain,
    post_gain,
    w_gate,
    w_up,
    w_down,
    final_gain,
    w_vocab,
):
    rows, width = tokens.shape
    head_dim = q_gain.shape[1]
    columns = w_qkv.shape[3]
    req = lax.axis_index(("y", "z"))
    ix, ic = lax.axis_index("x"), lax.axis_index("c")

    qkv_block = lax.all_gather(w_qkv[0, :, 0], "y", axis=0, tiled=True)
    out_part = lax.all_gather(w_out[0].T, "z", axis=0, tiled=True)
    out_block = lax.all_gather(out_part, "y", axis=0, tiled=True)
    gate_up = jnp.concatenate([w_gate[0].T, w_up[0].T], axis=0)
    gate_up = lax.all_gather(gate_up, "x", axis=0)
    down = lax.all_gather(w_down[0], "x", axis=0)

    positions = lax.dynamic_slice_in_dim(lengths, req * rows, rows)
    starts = jnp.cumsum(positions) - positions
    limits = starts + positions

    normed = rms_scale(tokens.astype(F32), in_gain[0]).astype(BF16)
    head_gate = jax.nn.sigmoid(jnp.dot(normed, w_headgate[0], preferred_element_type=F32))

    depth = width // (Y * Z)
    sent = normed.reshape(rows, Y, Z, depth).transpose(2, 0, 1, 3).reshape(Z, rows, Y * depth)
    arrived = swap(sent, "z").reshape(Z * rows, Y * depth)
    part = jnp.dot(arrived, qkv_block, preferred_element_type=F32).astype(BF16)
    qkv = jnp.sum(swap(part.reshape(Z, rows, columns), "z").astype(F32), axis=0)

    half = head_dim // 2
    frequency = ROPE_THETA ** (-2.0 * jnp.arange(half, dtype=F32) / head_dim)
    angles = positions.astype(F32)[:, None] * frequency[None, :]
    cosine, sine = jnp.cos(angles), jnp.sin(angles)
    query = qkv[:, : 2 * head_dim].reshape(rows, 2, head_dim)
    query = rotate(rms_scale(query, q_gain[0]), cosine[:, None], sine[:, None]).astype(BF16)
    key = qkv[:, 2 * head_dim : 3 * head_dim]
    key = rotate(rms_scale(key, k_gain[0]), cosine, sine).astype(BF16)
    value = qkv[:, 3 * head_dim :].astype(BF16)

    scale = head_dim ** (-0.5)
    keys, values = kv_cache[0, 0, :, 0], kv_cache[0, 1, :, 0]
    slots = keys.shape[0]
    score = jnp.einsum("rqd,sd->rqs", query, keys, preferred_element_type=F32) * scale
    slot = jnp.arange(slots, dtype=jnp.int32)
    inside = (slot[None, :] >= starts[:, None]) & (slot[None, :] < limits[:, None])
    weight = jnp.where(inside[:, None, :], jnp.exp(score), 0.0)
    own = jnp.exp(jnp.sum(query.astype(F32) * key.astype(F32)[:, None], axis=-1) * scale)
    total = jnp.sum(weight, axis=-1) + own
    summed = jnp.einsum("rqs,sd->rqd", weight.astype(BF16), values, preferred_element_type=F32)
    summed = summed + own.astype(BF16).astype(F32)[..., None] * value.astype(F32)[:, None]
    attended = summed / total[..., None]
    mixed = (attended * head_gate[..., None]).astype(BF16).reshape(rows, 2 * head_dim)

    part = lax.dot_general(mixed, out_block, (((1,), (1,)), ((), ())), preferred_element_type=F32)
    projected = jnp.sum(spread(part, ("x", "c"), X * C), axis=0)
    stream = (tokens.astype(F32) + projected).astype(BF16)
    normed_two = rms_scale(stream.astype(F32), post_gain[0]).astype(BF16)

    def mine(array):
        row = lax.dynamic_slice_in_dim(array, ix, 1, 0).reshape(X, C, width // (X * C))
        return lax.dynamic_slice_in_dim(row, ic, 1, 1).reshape(1, width // C)

    batch = spread(mine(normed_two), ("y", "z"), Y * Z).reshape(Y * Z, width // C)
    gate_up = gate_up.transpose(1, 0, 2).reshape(gate_up.shape[1], width // C)
    part = lax.dot_general(batch, gate_up, (((1,), (1,)), ((), ())), preferred_element_type=F32)
    both = jnp.sum(lax.all_gather(part, "c", axis=0), axis=0)
    units = w_gate.shape[2]
    hidden = (jax.nn.silu(both[:, :units]) * both[:, units:]).astype(BF16)
    down = down.transpose(1, 0, 2).reshape(units, width // C)
    part = jnp.dot(hidden, down, preferred_element_type=F32).astype(BF16)
    lowered = jnp.sum(swap(part.reshape(Y * Z, 1, width // C), ("y", "z")).astype(F32), axis=0)
    piece = (mine(stream).astype(F32) + lowered).astype(BF16)

    piece = spread(piece, ("y", "z"), Y * Z).reshape(Y * Z, width // C)
    piece = spread(piece, "x", X).reshape(X * Y * Z, width // C)
    whole = lax.all_gather(piece, "c", axis=0)
    mean_square = jnp.sum(jnp.square(whole.astype(F32)), axis=(0, 2)) / width
    gain = final_gain.reshape(X, C, width // (X * C)).transpose(1, 0, 2).reshape(C, 1, width // C)
    final = (whole.astype(F32) * lax.rsqrt(mean_square + EPSILON)[None, :, None] * gain).astype(BF16)
    vocab = w_vocab.reshape(X, C, width // (X * C), w_vocab.shape[1]).transpose(1, 0, 2, 3)
    vocab = vocab.reshape(C, width // C, w_vocab.shape[1])
    logits = jnp.dot(final[0], vocab[0], preferred_element_type=F32)
    logits = logits + jnp.dot(final[1], vocab[1], preferred_element_type=F32)
    logits = logits.astype(BF16).reshape(X, Y * Z, w_vocab.shape[1]).transpose(1, 0, 2)
    return logits.reshape(X * Y * Z, w_vocab.shape[1])


def solution(mesh):
    fine = Mesh(mesh.devices.reshape(Y, Z, X, C), ("y", "z", "x", "c"))
    req, head = ("y", "z"), ("x", "c")
    in_specs = (
        P(req, None),
        P(),
        P(None, None, req, head, None),
        P(None, req, head, None),
        P(None, None, head),
        P(None, head, req),
        P(),
        P(),
        P(),
        P(),
        P(None, head, req),
        P(None, head, req),
        P(None, req, head),
        P(),
        P(None, req + head),
    )
    out_specs = P(None, req + head)
    return jax.shard_map(local, mesh=fine, in_specs=in_specs, out_specs=out_specs, check_vma=False)
```

```python
import jax
import jax.numpy as jnp
from jax import lax
from jax.sharding import Mesh
from jax.sharding import PartitionSpec as P

EPSILON = 1e-06
ROPE_THETA = 1000000.0
Y, Z, X, C = 4, 16, 4, 2
F32, BF16 = jnp.float32, jnp.bfloat16


def rms_scale(values, gain):
    mean_square = jnp.mean(values * values, axis=-1, keepdims=True)
    return values * lax.rsqrt(mean_square + EPSILON) * gain


def rotate(values, cosine, sine):
    half = values.shape[-1] // 2
    a, b = values[..., :half], values[..., half:]
    return jnp.concatenate([a * cosine - b * sine, b * cosine + a * sine], axis=-1)


def swap(values, axes):
    return lax.all_to_all(values, axes, split_axis=0, concat_axis=0, tiled=True)


def spread(values, axes, count):
    return swap(jnp.broadcast_to(values[None], (count,) + values.shape), axes)


def local(
    tokens,
    lengths,
    kv_cache,
    w_qkv,
    w_headgate,
    w_out,
    in_gain,
    q_gain,
    k_gain,
    post_gain,
    w_gate,
    w_up,
    w_down,
    final_gain,
    w_vocab,
):
    rows, width = tokens.shape
    head_dim = q_gain.shape[1]
    columns = w_qkv.shape[3]
    units = w_gate.shape[2]
    seg = width // (X * C)
    part_width = width // C
    req = lax.axis_index(("y", "z"))
    ix, ic = lax.axis_index("x"), lax.axis_index("c")

    ffn = jnp.concatenate([w_gate[0].T, w_up[0].T, w_down[0]], axis=0)
    ffn = lax.all_gather(ffn, ("y", "x"), axis=0).reshape(Y, X, -1, seg)
    qkv_block = spread(w_qkv[0, :, 0], "y", Y).reshape(-1, columns)

    positions = lax.dynamic_slice_in_dim(lengths, req * rows, rows)
    starts = jnp.cumsum(positions) - positions
    limits = starts + positions

    normed = rms_scale(tokens.astype(F32), in_gain[0]).astype(BF16)
    head_gate = jax.nn.sigmoid(jnp.dot(normed, w_headgate[0], preferred_element_type=F32))

    depth = width // (Y * Z)
    sent = normed.reshape(rows, Y, Z, depth).transpose(2, 0, 1, 3).reshape(Z, rows, Y * depth)
    block = w_out[0].T
    block = jnp.concatenate([block[:, :head_dim], block[:, head_dim:]], axis=0)
    sent = jnp.concatenate(
        [sent, jnp.zeros((Z, 8 - rows, head_dim), BF16), jnp.broadcast_to(block[None], (Z,) + block.shape)], axis=1
    )
    arrived = swap(sent, "z")
    batch = arrived[:, :rows].reshape(Z * rows, Y * depth)
    out_block = arrived[:, 8:].reshape(Z, 2, -1, head_dim).transpose(1, 0, 2, 3).reshape(2, -1, head_dim)
    part = jnp.dot(batch, qkv_block, preferred_element_type=F32).astype(BF16)
    qkv = jnp.sum(swap(part.reshape(Z, rows, columns), "z").astype(F32), axis=0)
    out_block = spread(out_block, "y", Y)

    half = head_dim // 2
    frequency = ROPE_THETA ** (-2.0 * jnp.arange(half, dtype=F32) / head_dim)
    angles = positions.astype(F32)[:, None] * frequency[None, :]
    cosine, sine = jnp.cos(angles), jnp.sin(angles)
    query = qkv[:, : 2 * head_dim].reshape(rows, 2, head_dim)
    query = rotate(rms_scale(query, q_gain[0]), cosine[:, None], sine[:, None]).astype(BF16)
    key = qkv[:, 2 * head_dim : 3 * head_dim]
    key = rotate(rms_scale(key, k_gain[0]), cosine, sine).astype(BF16)
    value = qkv[:, 3 * head_dim :].astype(BF16)

    scale = head_dim ** (-0.5)
    keys, values = kv_cache[0, 0, :, 0], kv_cache[0, 1, :, 0]
    slots = keys.shape[0]
    score = jnp.einsum("rqd,sd->rqs", query, keys, preferred_element_type=F32) * scale
    slot = jnp.arange(slots, dtype=jnp.int32)
    inside = (slot[None, :] >= starts[:, None]) & (slot[None, :] < limits[:, None])
    weight = jnp.where(inside[:, None, :], jnp.exp(score), 0.0)
    own = jnp.exp(jnp.sum(query.astype(F32) * key.astype(F32)[:, None], axis=-1) * scale)
    total = jnp.sum(weight, axis=-1) + own
    summed = jnp.einsum("rqs,sd->rqd", weight.astype(BF16), values, preferred_element_type=F32)
    summed = summed + own.astype(BF16).astype(F32)[..., None] * value.astype(F32)[:, None]
    attended = summed / total[..., None]
    mixed = (attended * head_gate[..., None]).astype(BF16)

    part = jnp.einsum("rqd,yqnd->ryn", mixed, out_block, preferred_element_type=F32)
    part = part.reshape(rows, Y, C, seg).transpose(0, 2, 1, 3).reshape(rows * C, 8, part_width // 8)
    projected = jnp.sum(swap(part, ("x", "c")), axis=0)

    def mine(array):
        row = lax.dynamic_slice_in_dim(array, ix, 1, 0).reshape(X, C, seg)
        return lax.dynamic_slice_in_dim(row, ic, 1, 1).reshape(8, part_width // 8)

    def half_of(gain):
        return lax.dynamic_slice_in_dim(gain.reshape(X, C, seg), ic, 1, 1).reshape(8, part_width // 8)

    stream = (mine(tokens).astype(F32) + projected).astype(BF16)
    wide = stream.astype(F32)
    squares = jnp.sum(lax.all_gather(jnp.sum(wide * wide).reshape(1, 1), "c", axis=0)) / width
    normed_two = (wide * lax.rsqrt(squares + EPSILON) * half_of(post_gain[0])).astype(BF16)

    batch = spread(normed_two, "z", Z).reshape(Z, X, seg)
    part = jnp.einsum("bxk,yxfk->byf", batch, ffn[:, :, : 2 * units], preferred_element_type=F32)
    part = part.reshape(Z, Y * 2 * units)
    both = jnp.sum(lax.all_gather(part, "c", axis=0), axis=0).reshape(Z, Y, 2 * units)
    hidden = (jax.nn.silu(both[..., :units]) * both[..., units:]).astype(BF16)
    down = ffn[:, :, 2 * units : 3 * units]
    part = jnp.einsum("byf,yxfk->bxk", hidden, down, preferred_element_type=F32).astype(BF16)
    lowered = jnp.sum(swap(part.reshape(Z, 8, part_width // 8), "z").astype(F32), axis=0)
    piece = (wide + lowered).astype(BF16)

    piece = spread(piece, "z", Z).reshape(Z, part_width)
    piece = spread(piece, ("y", "x"), Y * X).reshape(Y * X * Z, part_width)
    whole = spread(piece, "c", C)
    mean_square = jnp.sum(jnp.square(whole.astype(F32)), axis=(0, 2)) / width
    gain = final_gain.reshape(X, C, seg).transpose(1, 0, 2).reshape(C, 1, part_width)
    final = (whole.astype(F32) * lax.rsqrt(mean_square + EPSILON)[None, :, None] * gain).astype(BF16)
    vocab = w_vocab.reshape(X, C, seg, w_vocab.shape[1]).transpose(1, 0, 2, 3)
    vocab = vocab.reshape(C, part_width, w_vocab.shape[1])
    logits = jnp.dot(final[0], vocab[0], preferred_element_type=F32)
    logits = logits + jnp.dot(final[1], vocab[1], preferred_element_type=F32)
    logits = logits.astype(BF16).reshape(Y, X, Z, w_vocab.shape[1]).transpose(0, 2, 1, 3)
    return logits.reshape(Y * X * Z, w_vocab.shape[1])


def solution(mesh):
    fine = Mesh(mesh.devices.reshape(Y, Z, X, C), ("y", "z", "x", "c"))
    req, head = ("y", "z"), ("x", "c")
    in_specs = (
        P(req, None),
        P(),
        P(None, None, req, head, None),
        P(None, req, head, None),
        P(None, None, head),
        P(None, head, req),
        P(),
        P(),
        P(),
        P(),
        P(None, head, req),
        P(None, head, req),
        P(None, req, head),
        P(),
        P(None, req + head),
    )
    out_specs = P(None, req + head)
    return jax.shard_map(local, mesh=fine, in_specs=in_specs, out_specs=out_specs, check_vma=False)
```

```python
import jax
import jax.numpy as jnp
from jax import lax
from jax.sharding import Mesh
from jax.sharding import PartitionSpec as P

EPSILON = 1e-06
ROPE_THETA = 1000000.0
Y, Z, X, C = 4, 16, 4, 2
F32, BF16 = jnp.float32, jnp.bfloat16


def rms_scale(values, gain):
    mean_square = jnp.mean(values * values, axis=-1, keepdims=True)
    return values * lax.rsqrt(mean_square + EPSILON) * gain


def rotate(values, cosine, sine):
    half = values.shape[-1] // 2
    a, b = values[..., :half], values[..., half:]
    return jnp.concatenate([a * cosine - b * sine, b * cosine + a * sine], axis=-1)


def swap(values, axes):
    return lax.all_to_all(values, axes, split_axis=0, concat_axis=0, tiled=True)


def spread(values, axes, count):
    return swap(jnp.broadcast_to(values[None], (count,) + values.shape), axes)


def local(
    tokens,
    lengths,
    kv_cache,
    w_qkv,
    w_headgate,
    w_out,
    in_gain,
    q_gain,
    k_gain,
    post_gain,
    w_gate,
    w_up,
    w_down,
    final_gain,
    w_vocab,
):
    rows, width = tokens.shape
    head_dim = q_gain.shape[1]
    columns = w_qkv.shape[3]
    units = w_gate.shape[2]
    seg = width // (X * C)
    part_width = width // C
    req = lax.axis_index(("y", "z"))
    ix, ic = lax.axis_index("x"), lax.axis_index("c")

    ffn = jnp.concatenate([w_gate[0].T, w_up[0].T, w_down[0]], axis=0)
    ffn = lax.all_gather(ffn, "x", axis=0).reshape(1, X, -1, seg)
    qkv_block = lax.all_gather(w_qkv[0, :, 0], "y", axis=0, tiled=True)

    positions = lax.dynamic_slice_in_dim(lengths, req * rows, rows)
    starts = jnp.cumsum(positions) - positions
    limits = starts + positions

    normed = rms_scale(tokens.astype(F32), in_gain[0]).astype(BF16)
    head_gate = jax.nn.sigmoid(jnp.dot(normed, w_headgate[0], preferred_element_type=F32))

    depth = width // (Y * Z)
    sent = normed.reshape(rows, Y, Z, depth).transpose(2, 0, 1, 3).reshape(Z, rows, Y * depth)
    block = w_out[0].T
    block = jnp.concatenate([block[:, :head_dim], block[:, head_dim:]], axis=0)
    sent = jnp.concatenate(
        [sent, jnp.zeros((Z, 8 - rows, head_dim), BF16), jnp.broadcast_to(block[None], (Z,) + block.shape)], axis=1
    )
    arrived = swap(sent, "z")
    batch = arrived[:, :rows].reshape(Z * rows, Y * depth)
    out_block = arrived[:, 8:].reshape(Z, 2, -1, head_dim).transpose(1, 0, 2, 3).reshape(2, -1, head_dim)
    part = jnp.dot(batch, qkv_block, preferred_element_type=F32).astype(BF16)
    qkv = jnp.sum(swap(part.reshape(Z, rows, columns), "z").astype(F32), axis=0)
    out_block = lax.all_gather(out_block, "y", axis=0)

    half = head_dim // 2
    frequency = ROPE_THETA ** (-2.0 * jnp.arange(half, dtype=F32) / head_dim)
    angles = positions.astype(F32)[:, None] * frequency[None, :]
    cosine, sine = jnp.cos(angles), jnp.sin(angles)
    query = qkv[:, : 2 * head_dim].reshape(rows, 2, head_dim)
    query = rotate(rms_scale(query, q_gain[0]), cosine[:, None], sine[:, None]).astype(BF16)
    key = qkv[:, 2 * head_dim : 3 * head_dim]
    key = rotate(rms_scale(key, k_gain[0]), cosine, sine).astype(BF16)
    value = qkv[:, 3 * head_dim :].astype(BF16)

    scale = head_dim ** (-0.5)
    keys, values = kv_cache[0, 0, :, 0], kv_cache[0, 1, :, 0]
    slots = keys.shape[0]
    score = jnp.einsum("rqd,sd->rqs", query, keys, preferred_element_type=F32) * scale
    slot = jnp.arange(slots, dtype=jnp.int32)
    inside = (slot[None, :] >= starts[:, None]) & (slot[None, :] < limits[:, None])
    weight = jnp.where(inside[:, None, :], jnp.exp(score), 0.0)
    own = jnp.exp(jnp.sum(query.astype(F32) * key.astype(F32)[:, None], axis=-1) * scale)
    total = jnp.sum(weight, axis=-1) + own
    summed = jnp.einsum("rqs,sd->rqd", weight.astype(BF16), values, preferred_element_type=F32)
    summed = summed + own.astype(BF16).astype(F32)[..., None] * value.astype(F32)[:, None]
    attended = summed / total[..., None]
    mixed = (attended * head_gate[..., None]).astype(BF16)

    part = jnp.einsum("rqd,yqnd->ryn", mixed, out_block, preferred_element_type=F32)
    part = part.reshape(rows, Y, C, seg).transpose(0, 2, 1, 3).reshape(rows * C, 8, part_width // 8)
    projected = jnp.sum(swap(part, ("x", "c")), axis=0)

    def mine(array):
        row = lax.dynamic_slice_in_dim(array, ix, 1, 0).reshape(X, C, seg)
        return lax.dynamic_slice_in_dim(row, ic, 1, 1).reshape(8, part_width // 8)

    def half_of(gain):
        return lax.dynamic_slice_in_dim(gain.reshape(X, C, seg), ic, 1, 1).reshape(8, part_width // 8)

    stream = (mine(tokens).astype(F32) + projected).astype(BF16)

    batch = spread(stream, ("y", "z"), Y * Z).reshape(Y * Z, part_width)
    wide = batch.astype(F32)
    squares = jnp.sum(wide * wide, axis=-1, keepdims=True)
    batch = (wide * half_of(post_gain[0]).reshape(1, part_width)).astype(BF16).reshape(Y * Z, X, seg)
    part = jnp.einsum("bxk,xfk->bf", batch, ffn[0, :, : 2 * units], preferred_element_type=F32)
    part = jnp.concatenate([part, jnp.broadcast_to(squares, (Y * Z, 256 - 2 * units))], axis=1)
    both = jnp.sum(lax.all_gather(part, "c", axis=0), axis=0)
    both = both[:, : 2 * units] * lax.rsqrt(both[:, 2 * units :][:, :1] / width + EPSILON)
    hidden = (jax.nn.silu(both[:, :units]) * both[:, units:]).astype(BF16)
    down = ffn[0, :, 2 * units :]
    part = jnp.einsum("bf,xfk->bxk", hidden, down, preferred_element_type=F32).astype(BF16)
    lowered = jnp.sum(swap(part.reshape((Y * Z), 8, part_width // 8), ("y", "z")).astype(F32), axis=0)
    piece = (stream.astype(F32) + lowered).astype(BF16)

    piece = spread(piece, "z", Z).reshape(Z, part_width)
    piece = spread(piece, ("y", "x"), Y * X).reshape(Y * X * Z, part_width)
    whole = spread(piece, "c", C)
    mean_square = jnp.sum(jnp.square(whole.astype(F32)), axis=(0, 2)) / width
    gain = final_gain.reshape(X, C, seg).transpose(1, 0, 2).reshape(C, 1, part_width)
    final = (whole.astype(F32) * lax.rsqrt(mean_square + EPSILON)[None, :, None] * gain).astype(BF16)
    vocab = w_vocab.reshape(X, C, seg, w_vocab.shape[1]).transpose(1, 0, 2, 3)
    vocab = vocab.reshape(C, part_width, w_vocab.shape[1])
    logits = jnp.dot(final[0], vocab[0], preferred_element_type=F32)
    logits = logits + jnp.dot(final[1], vocab[1], preferred_element_type=F32)
    logits = logits.astype(BF16).reshape(Y, X, Z, w_vocab.shape[1]).transpose(0, 2, 1, 3)
    return logits.reshape(Y * X * Z, w_vocab.shape[1])


def solution(mesh):
    fine = Mesh(mesh.devices.reshape(Y, Z, X, C), ("y", "z", "x", "c"))
    req, head = ("y", "z"), ("x", "c")
    in_specs = (
        P(req, None),
        P(),
        P(None, None, req, head, None),
        P(None, req, head, None),
        P(None, None, head),
        P(None, head, req),
        P(),
        P(),
        P(),
        P(),
        P(None, head, req),
        P(None, head, req),
        P(None, req, head),
        P(),
        P(None, req + head),
    )
    out_specs = P(None, req + head)
    return jax.shard_map(local, mesh=fine, in_specs=in_specs, out_specs=out_specs, check_vma=False)
```

```python
import jax
import jax.numpy as jnp
from jax import lax
from jax.sharding import Mesh
from jax.sharding import PartitionSpec as P

EPSILON = 1e-06
ROPE_THETA = 1000000.0
Y, Z, X, C = 4, 16, 4, 2
F32, BF16 = jnp.float32, jnp.bfloat16


def rms_scale(values, gain):
    mean_square = jnp.mean(values * values, axis=-1, keepdims=True)
    return values * lax.rsqrt(mean_square + EPSILON) * gain


def rotate(values, cosine, sine):
    half = values.shape[-1] // 2
    a, b = values[..., :half], values[..., half:]
    return jnp.concatenate([a * cosine - b * sine, b * cosine + a * sine], axis=-1)


def swap(values, axes):
    return lax.all_to_all(values, axes, split_axis=0, concat_axis=0, tiled=True)


def spread(values, axes, count):
    return swap(jnp.broadcast_to(values[None], (count,) + values.shape), axes)


def local(
    tokens,
    lengths,
    kv_cache,
    w_qkv,
    w_headgate,
    w_out,
    in_gain,
    q_gain,
    k_gain,
    post_gain,
    w_gate,
    w_up,
    w_down,
    final_gain,
    w_vocab,
):
    rows, width = tokens.shape
    head_dim = q_gain.shape[1]
    columns = w_qkv.shape[3]
    units = w_gate.shape[2]
    seg = width // (X * C)
    part_width = width // C
    req = lax.axis_index(("y", "z"))
    ix, ic = lax.axis_index("x"), lax.axis_index("c")

    ffn = jnp.concatenate([w_gate[0].T, w_up[0].T, w_down[0]], axis=0)
    ffn = lax.all_gather(ffn, ("y", "x"), axis=0).reshape(Y, X, -1, seg)
    qkv_block = lax.all_gather(w_qkv[0, :, 0], "y", axis=0, tiled=True)

    positions = lax.dynamic_slice_in_dim(lengths, req * rows, rows)
    starts = jnp.cumsum(positions) - positions
    limits = starts + positions

    normed = rms_scale(tokens.astype(F32), in_gain[0]).astype(BF16)
    head_gate = jax.nn.sigmoid(jnp.dot(normed, w_headgate[0], preferred_element_type=F32))

    depth = width // (Y * Z)
    sent = normed.reshape(rows, Y, Z, depth).transpose(2, 0, 1, 3).reshape(Z, rows, Y * depth)
    block = w_out[0].T
    block = jnp.concatenate([block[:, :head_dim], block[:, head_dim:]], axis=0)
    sent = jnp.concatenate(
        [sent, jnp.zeros((Z, 8 - rows, head_dim), BF16), jnp.broadcast_to(block[None], (Z,) + block.shape)], axis=1
    )
    arrived = swap(sent, "z")
    batch = arrived[:, :rows].reshape(Z * rows, Y * depth)
    out_block = arrived[:, 8:].reshape(Z, 2, -1, head_dim)
    part = jnp.dot(batch, qkv_block, preferred_element_type=F32).astype(BF16)
    qkv = jnp.sum(swap(part.reshape(Z, rows, columns), "z").astype(F32), axis=0)

    half = head_dim // 2
    frequency = ROPE_THETA ** (-2.0 * jnp.arange(half, dtype=F32) / head_dim)
    angles = positions.astype(F32)[:, None] * frequency[None, :]
    cosine, sine = jnp.cos(angles), jnp.sin(angles)
    query = qkv[:, : 2 * head_dim].reshape(rows, 2, head_dim)
    query = rotate(rms_scale(query, q_gain[0]), cosine[:, None], sine[:, None]).astype(BF16)
    key = qkv[:, 2 * head_dim : 3 * head_dim]
    key = rotate(rms_scale(key, k_gain[0]), cosine, sine).astype(BF16)
    value = qkv[:, 3 * head_dim :].astype(BF16)

    scale = head_dim ** (-0.5)
    keys, values = kv_cache[0, 0, :, 0], kv_cache[0, 1, :, 0]
    slots = keys.shape[0]
    score = jnp.einsum("rqd,sd->rqs", query, keys, preferred_element_type=F32) * scale
    slot = jnp.arange(slots, dtype=jnp.int32)
    inside = (slot[None, :] >= starts[:, None]) & (slot[None, :] < limits[:, None])
    weight = jnp.where(inside[:, None, :], jnp.exp(score), 0.0)
    own = jnp.exp(jnp.sum(query.astype(F32) * key.astype(F32)[:, None], axis=-1) * scale)
    total = jnp.sum(weight, axis=-1) + own
    summed = jnp.einsum("rqs,sd->rqd", weight.astype(BF16), values, preferred_element_type=F32)
    summed = summed + own.astype(BF16).astype(F32)[..., None] * value.astype(F32)[:, None]
    attended = summed / total[..., None]
    mixed = (attended * head_gate[..., None]).astype(BF16)

    def own_row(array):
        return lax.dynamic_slice_in_dim(array, ix, 1, 0)

    def own_core(array, axis):
        return lax.dynamic_slice_in_dim(array, ic, 1, axis)

    residual = own_core(own_row(tokens).reshape(Y, C, seg), 1).reshape(Y, 2, head_dim)
    sent = jnp.broadcast_to(mixed.transpose(1, 0, 2).reshape(1, 2 * rows, head_dim), (Y, 2 * rows, head_dim))
    sent = jnp.concatenate([sent, residual, jnp.zeros((Y, 6, head_dim), BF16)], axis=1)
    arrived = swap(sent, "y")
    everyone = arrived[:, : 2 * rows].reshape(Y, 2, rows, head_dim)
    residual = arrived[:, 2 * rows : 2 * rows + 2].reshape(8, head_dim)
    part = jnp.einsum("yqrd,zqnd->yrzn", everyone, out_block, preferred_element_type=F32)
    part = part.reshape(Y, rows, C, seg).transpose(1, 2, 0, 3).reshape(rows * C, 8, head_dim)
    projected = jnp.sum(swap(part, ("x", "c")), axis=0)
    stream = (residual.astype(F32) + projected).astype(BF16).reshape(Y, 2, head_dim)

    sent = jnp.broadcast_to(stream[:, None], (Y, Z, 2, head_dim)).reshape(Y * Z, 2, head_dim)
    batch = swap(sent, ("y", "z")).reshape(Y, Z, seg).transpose(1, 0, 2)
    stream = lax.dynamic_slice_in_dim(batch, lax.axis_index("z"), 1, 0).reshape(8, head_dim)
    wide = batch.astype(F32)
    squares = jnp.sum(wide * wide, axis=(1, 2)).reshape(Z, 1)
    batch = (wide * own_core(post_gain.reshape(X, C, seg), 1).reshape(X, seg)).astype(BF16)
    part = jnp.einsum("bxk,yxfk->byf", batch, ffn[:, :, : 2 * units], preferred_element_type=F32)
    part = jnp.concatenate([part.reshape(Z, -1), jnp.broadcast_to(squares, (Z, head_dim))], axis=1)
    both = jnp.sum(lax.all_gather(part, "c", axis=0), axis=0)
    scale = lax.rsqrt(both[:, -1:] / width + EPSILON)
    both = (both[:, :-head_dim] * scale).reshape(Z, Y, 2 * units)
    hidden = (jax.nn.silu(both[..., :units]) * both[..., units:]).astype(BF16)
    down = ffn[:, :, 2 * units : 3 * units]
    part = jnp.einsum("byf,yxfk->bxk", hidden, down, preferred_element_type=F32).astype(BF16)
    lowered = jnp.sum(swap(part.reshape(Z, 8, part_width // 8), "z").astype(F32), axis=0)
    piece = (stream.astype(F32) + lowered).astype(BF16)

    piece = spread(piece, "z", Z).reshape(Z, part_width)
    piece = spread(piece, ("y", "x"), Y * X).reshape(Y * X * Z, part_width)
    whole = spread(piece, "c", C)
    mean_square = jnp.sum(jnp.square(whole.astype(F32)), axis=(0, 2)) / width
    gain = final_gain.reshape(X, C, seg).transpose(1, 0, 2).reshape(C, 1, part_width)
    final = (whole.astype(F32) * lax.rsqrt(mean_square + EPSILON)[None, :, None] * gain).astype(BF16)
    vocab = w_vocab.reshape(X, C, seg, w_vocab.shape[1]).transpose(1, 0, 2, 3)
    vocab = vocab.reshape(C, part_width, w_vocab.shape[1])
    logits = jnp.dot(final[0], vocab[0], preferred_element_type=F32)
    logits = logits + jnp.dot(final[1], vocab[1], preferred_element_type=F32)
    logits = logits.astype(BF16).reshape(Y, X, Z, w_vocab.shape[1]).transpose(0, 2, 1, 3)
    return logits.reshape(Y * X * Z, w_vocab.shape[1])


def solution(mesh):
    fine = Mesh(mesh.devices.reshape(Y, Z, X, C), ("y", "z", "x", "c"))
    req, head = ("y", "z"), ("x", "c")
    in_specs = (
        P(req, None),
        P(),
        P(None, None, req, head, None),
        P(None, req, head, None),
        P(None, None, head),
        P(None, head, req),
        P(),
        P(),
        P(),
        P(),
        P(None, head, req),
        P(None, head, req),
        P(None, req, head),
        P(),
        P(None, req + head),
    )
    out_specs = P(None, req + head)
    return jax.shard_map(local, mesh=fine, in_specs=in_specs, out_specs=out_specs, check_vma=False)
```

```python
import jax
import jax.numpy as jnp
from jax import lax
from jax.sharding import Mesh
from jax.sharding import PartitionSpec as P

EPSILON = 1e-06
ROPE_THETA = 1000000.0
Y, Z, X, C = 4, 16, 4, 2
F32, BF16 = jnp.float32, jnp.bfloat16


def rms_scale(values, gain):
    mean_square = jnp.mean(values * values, axis=-1, keepdims=True)
    return values * lax.rsqrt(mean_square + EPSILON) * gain


def rotate(values, cosine, sine):
    half = values.shape[-1] // 2
    a, b = values[..., :half], values[..., half:]
    return jnp.concatenate([a * cosine - b * sine, b * cosine + a * sine], axis=-1)


def swap(values, axes):
    return lax.all_to_all(values, axes, split_axis=0, concat_axis=0, tiled=True)


def spread(values, axes, count):
    return swap(jnp.broadcast_to(values[None], (count,) + values.shape), axes)


def local(
    tokens,
    lengths,
    kv_cache,
    w_qkv,
    w_headgate,
    w_out,
    in_gain,
    q_gain,
    k_gain,
    post_gain,
    w_gate,
    w_up,
    w_down,
    final_gain,
    w_vocab,
):
    rows, width = tokens.shape
    head_dim = q_gain.shape[1]
    columns = w_qkv.shape[3]
    units = w_gate.shape[2]
    seg = width // (X * C)
    part_width = width // C
    req = lax.axis_index(("y", "z"))
    ix, ic = lax.axis_index("x"), lax.axis_index("c")

    ffn = jnp.concatenate([w_gate[0].T, w_up[0].T, w_down[0]], axis=0)
    ffn = lax.all_gather(ffn, ("y", "x"), axis=0).reshape(Y, X, -1, seg)
    qkv_block = lax.all_gather(w_qkv[0, :, 0], "y", axis=0, tiled=True)

    positions = lax.dynamic_slice_in_dim(lengths, req * rows, rows)
    starts = jnp.cumsum(positions) - positions
    limits = starts + positions

    normed = rms_scale(tokens.astype(F32), in_gain[0]).astype(BF16)
    head_gate = jax.nn.sigmoid(jnp.dot(normed, w_headgate[0], preferred_element_type=F32))

    depth = width // (Y * Z)
    sent = normed.reshape(rows, Y, Z, depth).transpose(2, 0, 1, 3).reshape(Z, rows, Y * depth)
    block = w_out[0].T
    block = jnp.concatenate([block[:, :head_dim], block[:, head_dim:]], axis=0)
    sent = jnp.concatenate(
        [sent, jnp.zeros((Z, 8 - rows, head_dim), BF16), jnp.broadcast_to(block[None], (Z,) + block.shape)], axis=1
    )
    arrived = swap(sent, "z")
    batch = arrived[:, :rows].reshape(Z * rows, Y * depth)
    out_block = arrived[:, 8:].reshape(Z, 2, -1, head_dim)
    part = jnp.dot(batch, qkv_block, preferred_element_type=F32).astype(BF16)
    qkv = jnp.sum(swap(part.reshape(Z, rows, columns), "z").astype(F32), axis=0)

    half = head_dim // 2
    frequency = ROPE_THETA ** (-2.0 * jnp.arange(half, dtype=F32) / head_dim)
    angles = positions.astype(F32)[:, None] * frequency[None, :]
    cosine, sine = jnp.cos(angles), jnp.sin(angles)
    query = qkv[:, : 2 * head_dim].reshape(rows, 2, head_dim)
    query = rotate(rms_scale(query, q_gain[0]), cosine[:, None], sine[:, None]).astype(BF16)
    key = qkv[:, 2 * head_dim : 3 * head_dim]
    key = rotate(rms_scale(key, k_gain[0]), cosine, sine).astype(BF16)
    value = qkv[:, 3 * head_dim :].astype(BF16)

    scale = head_dim ** (-0.5)
    keys, values = kv_cache[0, 0, :, 0], kv_cache[0, 1, :, 0]
    slots = keys.shape[0]
    score = jnp.einsum("rqd,sd->rqs", query, keys, preferred_element_type=F32) * scale
    slot = jnp.arange(slots, dtype=jnp.int32)
    inside = (slot[None, :] >= starts[:, None]) & (slot[None, :] < limits[:, None])
    weight = jnp.where(inside[:, None, :], jnp.exp(score), 0.0)
    own = jnp.exp(jnp.sum(query.astype(F32) * key.astype(F32)[:, None], axis=-1) * scale)
    total = jnp.sum(weight, axis=-1) + own
    summed = jnp.einsum("rqs,sd->rqd", weight.astype(BF16), values, preferred_element_type=F32)
    summed = summed + own.astype(BF16).astype(F32)[..., None] * value.astype(F32)[:, None]
    attended = summed / total[..., None]
    mixed = (attended * head_gate[..., None]).astype(BF16)

    def own_row(array):
        return lax.dynamic_slice_in_dim(array, ix, 1, 0)

    def own_core(array, axis):
        return lax.dynamic_slice_in_dim(array, ic, 1, axis)

    residual = own_core(own_row(tokens).reshape(Y, C, seg), 1).reshape(8, head_dim)
    everyone = spread(mixed.transpose(1, 0, 2).reshape(2 * rows, head_dim), "y", Y).reshape(Y, 2, rows, head_dim)
    part = jnp.einsum("yqrd,zqnd->yrzn", everyone, out_block, preferred_element_type=F32)
    part = swap(part.reshape(Y * rows * C, 2, head_dim), ("y", "x", "c"))
    projected = jnp.sum(part.reshape(Y, X * C, 2, head_dim), axis=1).reshape(8, head_dim)
    stream = (residual.astype(F32) + projected).astype(BF16)

    batch = spread(stream, "z", Z).reshape(Z, X, seg)
    wide = batch.astype(F32)
    squares = jnp.sum(wide * wide, axis=(1, 2)).reshape(Z, 1)
    batch = (wide * own_core(post_gain.reshape(X, C, seg), 1).reshape(X, seg)).astype(BF16)
    part = jnp.einsum("bxk,yxfk->byf", batch, ffn[:, :, : 2 * units], preferred_element_type=F32)
    part = jnp.concatenate([part.reshape(Z, -1), jnp.broadcast_to(squares, (Z, head_dim))], axis=1)
    both = jnp.sum(lax.all_gather(part, "c", axis=0), axis=0)
    scale = lax.rsqrt(both[:, -1:] / width + EPSILON)
    both = (both[:, :-head_dim] * scale).reshape(Z, Y, 2 * units)
    hidden = (jax.nn.silu(both[..., :units]) * both[..., units:]).astype(BF16)
    down = ffn[:, :, 2 * units : 3 * units]
    part = jnp.einsum("byf,yxfk->bxk", hidden, down, preferred_element_type=F32).astype(BF16)
    lowered = jnp.sum(spread(part.reshape(Z, 8, head_dim), "z", Z).astype(F32), axis=0)
    piece = (wide.reshape(Z, 8, head_dim) + lowered).astype(BF16).reshape(Z, part_width)

    near = spread(piece, ("y", "x"), Y * X).reshape(Y * X * Z, part_width)
    far = lax.ppermute(near, "c", [(0, 1), (1, 0)])
    near, far = near.astype(F32), far.astype(F32)
    mean_square = (jnp.sum(near * near, axis=-1, keepdims=True) + jnp.sum(far * far, axis=-1, keepdims=True)) / width
    scale = lax.rsqrt(mean_square + EPSILON)

    def scored(half, core):
        gain = lax.dynamic_slice_in_dim(final_gain.reshape(X, C, seg), core, 1, 1).reshape(1, part_width)
        vocab = lax.dynamic_slice_in_dim(w_vocab.reshape(X, C, seg, -1), core, 1, 1).reshape(part_width, -1)
        return jnp.dot((half * scale * gain).astype(BF16), vocab, preferred_element_type=F32)

    logits = (scored(near, ic) + scored(far, 1 - ic)).astype(BF16)
    logits = logits.reshape(Y, X, Z, w_vocab.shape[1]).transpose(0, 2, 1, 3)
    return logits.reshape(Y * X * Z, w_vocab.shape[1])


def solution(mesh):
    fine = Mesh(mesh.devices.reshape(Y, Z, X, C), ("y", "z", "x", "c"))
    req, head = ("y", "z"), ("x", "c")
    in_specs = (
        P(req, None),
        P(),
        P(None, None, req, head, None),
        P(None, req, head, None),
        P(None, None, head),
        P(None, head, req),
        P(),
        P(),
        P(),
        P(),
        P(None, head, req),
        P(None, head, req),
        P(None, req, head),
        P(),
        P(None, req + head),
    )
    out_specs = P(None, req + head)
    return jax.shard_map(local, mesh=fine, in_specs=in_specs, out_specs=out_specs, check_vma=False)
```

```python
import jax
import jax.numpy as jnp
from jax import lax
from jax.sharding import Mesh
from jax.sharding import PartitionSpec as P

EPSILON = 1e-06
ROPE_THETA = 1000000.0
Y, Z, X, C = 4, 16, 4, 2
F32, BF16 = jnp.float32, jnp.bfloat16


def rms_scale(values, gain):
    mean_square = jnp.mean(values * values, axis=-1, keepdims=True)
    return values * lax.rsqrt(mean_square + EPSILON) * gain


def rotate(values, cosine, sine):
    half = values.shape[-1] // 2
    a, b = values[..., :half], values[..., half:]
    return jnp.concatenate([a * cosine - b * sine, b * cosine + a * sine], axis=-1)


def swap(values, axes):
    return lax.all_to_all(values, axes, split_axis=0, concat_axis=0, tiled=True)


def spread(values, axes, count):
    return swap(jnp.broadcast_to(values[None], (count,) + values.shape), axes)


def local(
    tokens,
    lengths,
    kv_cache,
    w_qkv,
    w_headgate,
    w_out,
    in_gain,
    q_gain,
    k_gain,
    post_gain,
    w_gate,
    w_up,
    w_down,
    final_gain,
    w_vocab,
):
    rows, width = tokens.shape
    head_dim = q_gain.shape[1]
    columns = w_qkv.shape[3]
    units = w_gate.shape[2]
    seg = width // (X * C)
    part_width = width // C
    req = lax.axis_index(("y", "z"))
    ix, ic = lax.axis_index("x"), lax.axis_index("c")

    ffn = jnp.concatenate([w_gate[0].T, w_up[0].T, w_down[0]], axis=0)
    ffn = lax.all_gather(ffn, ("y", "x"), axis=0).reshape(Y, X, -1, seg)
    qkv_block = lax.all_gather(w_qkv[0, :, 0], "y", axis=0, tiled=True)

    positions = lax.dynamic_slice_in_dim(lengths, req * rows, rows)
    starts = jnp.cumsum(positions) - positions
    limits = starts + positions

    normed = rms_scale(tokens.astype(F32), in_gain[0]).astype(BF16)
    head_gate = jax.nn.sigmoid(jnp.dot(normed, w_headgate[0], preferred_element_type=F32))

    half = head_dim // 2
    frequency = ROPE_THETA ** (-2.0 * jnp.arange(half, dtype=F32) / head_dim)
    angles = positions.astype(F32)[:, None] * frequency[None, :]
    cosine, sine = jnp.cos(angles), jnp.sin(angles)

    def own_row(array):
        return lax.dynamic_slice_in_dim(array, ix, 1, 0)

    def own_core(array, axis):
        return lax.dynamic_slice_in_dim(array, ic, 1, axis)

    residual = own_core(own_row(tokens).reshape(Y, C, seg), 1).reshape(8, head_dim)
    post_half = own_core(post_gain.reshape(X, C, seg), 1).reshape(X, seg)
    slot = jnp.arange(kv_cache.shape[2], dtype=jnp.int32)
    inside = (slot[None, :] >= starts[:, None]) & (slot[None, :] < limits[:, None])
    inside = inside.astype(F32)

    depth = width // (Y * Z)
    sent = normed.reshape(rows, Y, Z, depth).transpose(2, 0, 1, 3).reshape(Z, rows, Y * depth)
    block = w_out[0].T
    block = jnp.concatenate([block[:, :head_dim], block[:, head_dim:]], axis=0)
    sent = jnp.concatenate(
        [sent, jnp.zeros((Z, 8 - rows, head_dim), BF16), jnp.broadcast_to(block[None], (Z,) + block.shape)], axis=1
    )
    arrived = swap(sent, "z")
    arrived, qkv_block, head_gate, cosine, sine, residual, post_half, inside = lax.optimization_barrier(
        (arrived, qkv_block, head_gate, cosine, sine, residual, post_half, inside)
    )
    batch = arrived[:, :rows].reshape(Z * rows, Y * depth)
    out_block = arrived[:, 8:].reshape(Z, 2, -1, head_dim).transpose(1, 0, 2, 3).reshape(2, -1, head_dim)
    part = jnp.dot(batch, qkv_block, preferred_element_type=F32).astype(BF16)
    part, out_block = lax.optimization_barrier((swap(part.reshape(Z, rows, columns), "z"), out_block))
    qkv = jnp.sum(part.astype(F32), axis=0)

    query = qkv[:, : 2 * head_dim].reshape(rows, 2, head_dim)
    query = rotate(rms_scale(query, q_gain[0]), cosine[:, None], sine[:, None]).astype(BF16)
    key = qkv[:, 2 * head_dim : 3 * head_dim]
    key = rotate(rms_scale(key, k_gain[0]), cosine, sine).astype(BF16)
    value = qkv[:, 3 * head_dim :].astype(BF16)

    scale = head_dim ** (-0.5)
    keys, values = kv_cache[0, 0, :, 0], kv_cache[0, 1, :, 0]
    score = jnp.einsum("rqd,sd->rqs", query, keys, preferred_element_type=F32) * scale
    weight = jnp.where(inside[:, None, :] > 0.0, jnp.exp(score), 0.0)
    own = jnp.exp(jnp.sum(query.astype(F32) * key.astype(F32)[:, None], axis=-1) * scale)
    total = jnp.sum(weight, axis=-1) + own
    summed = jnp.einsum("rqs,sd->rqd", weight.astype(BF16), values, preferred_element_type=F32)
    summed = summed + own.astype(BF16).astype(F32)[..., None] * value.astype(F32)[:, None]
    attended = summed / total[..., None]
    mixed = (attended * head_gate[..., None]).astype(BF16)

    everyone = spread(mixed.transpose(1, 0, 2).reshape(2 * rows, head_dim), "y", Y).reshape(Y, 2, rows, head_dim)
    part = jnp.einsum("yqrd,qnd->yrn", everyone, out_block, preferred_element_type=F32)
    part = swap(part.reshape(Y * rows * C, 2, head_dim), ("y", "x", "c"))
    projected = jnp.sum(part.reshape(Y, X * C, 2, head_dim), axis=1).reshape(8, head_dim)
    stream = (residual.astype(F32) + projected).astype(BF16)

    batch = spread(stream, "z", Z).reshape(Z, X, seg)
    wide = batch.astype(F32)
    squares = jnp.sum(wide * wide, axis=(1, 2)).reshape(Z, 1)
    batch = (wide * post_half).astype(BF16)
    part = jnp.einsum("bxk,yxfk->byf", batch, ffn[:, :, : 2 * units], preferred_element_type=F32)
    part = jnp.concatenate([part.reshape(Z, -1), jnp.broadcast_to(squares, (Z, head_dim))], axis=1)
    both = jnp.sum(lax.all_gather(part, "c", axis=0), axis=0)
    scale = lax.rsqrt(both[:, -1:] / width + EPSILON)
    both = (both[:, :-head_dim] * scale).reshape(Z, Y, 2 * units)
    hidden = (jax.nn.silu(both[..., :units]) * both[..., units:]).astype(BF16)
    down = ffn[:, :, 2 * units : 3 * units]
    part = jnp.einsum("byf,yxfk->bxk", hidden, down, preferred_element_type=F32).astype(BF16)
    lowered = jnp.sum(swap(part.reshape(Z, 8, head_dim), "z").astype(F32), axis=0)
    piece = (stream.astype(F32) + lowered).astype(BF16)

    piece = spread(piece, "z", Z).reshape(Z, part_width)
    near = spread(piece, ("y", "x"), Y * X).reshape(Y * X * Z, part_width)
    far = lax.ppermute(near, "c", [(0, 1), (1, 0)])
    near, far = near.astype(F32), far.astype(F32)
    mean_square = (jnp.sum(near * near, axis=-1, keepdims=True) + jnp.sum(far * far, axis=-1, keepdims=True)) / width
    scale = lax.rsqrt(mean_square + EPSILON)

    def scored(half, core):
        gain = lax.dynamic_slice_in_dim(final_gain.reshape(X, C, seg), core, 1, 1).reshape(1, part_width)
        vocab = lax.dynamic_slice_in_dim(w_vocab.reshape(X, C, seg, -1), core, 1, 1).reshape(part_width, -1)
        return jnp.dot((half * scale * gain).astype(BF16), vocab, preferred_element_type=F32)

    logits = (scored(near, ic) + scored(far, 1 - ic)).astype(BF16)
    logits = logits.reshape(Y, X, Z, w_vocab.shape[1]).transpose(0, 2, 1, 3)
    return logits.reshape(Y * X * Z, w_vocab.shape[1])


def solution(mesh):
    fine = Mesh(mesh.devices.reshape(Y, Z, X, C), ("y", "z", "x", "c"))
    req, head = ("y", "z"), ("x", "c")
    in_specs = (
        P(req, None),
        P(),
        P(None, None, req, head, None),
        P(None, req, head, None),
        P(None, None, head),
        P(None, head, req),
        P(),
        P(),
        P(),
        P(),
        P(None, head, req),
        P(None, head, req),
        P(None, req, head),
        P(),
        P(None, req + head),
    )
    out_specs = P(None, req + head)
    return jax.shard_map(local, mesh=fine, in_specs=in_specs, out_specs=out_specs, check_vma=False)
```

```python
import jax
import jax.numpy as jnp
from jax import lax
from jax.experimental import pallas as pl
from jax.experimental.pallas import tpu as pltpu
from jax.sharding import Mesh
from jax.sharding import PartitionSpec as P

EPSILON = 1e-06
ROPE_THETA = 1000000.0
Y, Z, X, C = 4, 16, 4, 2
F32, BF16 = jnp.float32, jnp.bfloat16


def rms_scale(values, gain):
    mean_square = jnp.mean(values * values, axis=-1, keepdims=True)
    return values * lax.rsqrt(mean_square + EPSILON) * gain


def rotate(values, cosine, sine):
    half = values.shape[-1] // 2
    a, b = values[..., :half], values[..., half:]
    return jnp.concatenate([a * cosine - b * sine, b * cosine + a * sine], axis=-1)


def swap(values, axes):
    return lax.all_to_all(values, axes, split_axis=0, concat_axis=0, tiled=True)


def spread(values, axes, count):
    return swap(jnp.broadcast_to(values[None], (count,) + values.shape), axes)


def first_kernel(tokens, gain, block, gate, up, down, sent, ffn, normed, token_buf, gain_buf, block_buf, sems):
    rows, width = token_buf.shape
    units = gate.shape[0]
    loads = [
        pltpu.make_async_copy(source, target, sems.at[i])
        for i, (source, target) in enumerate(((tokens, token_buf), (gain, gain_buf), (block, block_buf)))
    ]
    moves = [
        pltpu.make_async_copy(source, ffn.at[pl.ds(i * units, units)], sems.at[3 + i])
        for i, source in enumerate((gate, up, down))
    ]
    for copy in loads + moves:
        copy.start()
    for copy in loads:
        copy.wait()
    wide = token_buf[...].astype(F32)
    scale = lax.rsqrt(jnp.sum(wide * wide, axis=-1, keepdims=True) / width + EPSILON)
    wide = wide * scale * gain_buf[...]
    normed[...] = wide.astype(BF16)
    span, depth = width // Y, width // (Y * Z)
    empty = jnp.zeros((8 - rows, Y * depth), F32)
    left, right = block_buf[:, : Y * depth], block_buf[:, Y * depth :]
    for z in range(Z):
        mine = [wide[:, y * span + z * depth : y * span + (z + 1) * depth] for y in range(Y)]
        head = jnp.concatenate([jnp.concatenate(mine, axis=1), empty], axis=0).astype(BF16)
        sent[z, :8] = head
        sent[z, 8 : 8 + depth] = left
        sent[z, 8 + depth :] = right
    for copy in moves:
        copy.wait()


def first(tokens, gain, block, gate, up, down):
    rows, width = tokens.shape
    depth = width // (Y * Z)
    anywhere = pl.BlockSpec(memory_space=pl.ANY)
    local = pl.BlockSpec(memory_space=pltpu.VMEM)
    return pl.pallas_call(
        first_kernel,
        out_shape=(
            jax.ShapeDtypeStruct((Z, 8 + 2 * depth, Y * depth), BF16),
            jax.ShapeDtypeStruct((3 * gate.shape[0], gate.shape[1]), BF16),
            jax.ShapeDtypeStruct((rows, width), BF16),
        ),
        in_specs=[anywhere] * 6,
        out_specs=(local, anywhere, local),
        scratch_shapes=[
            pltpu.VMEM((rows, width), BF16),
            pltpu.VMEM((1, width), F32),
            pltpu.VMEM(block.shape, BF16),
            pltpu.SemaphoreType.DMA((6,)),
        ],
        name="first",
    )(tokens, gain, block, gate, up, down)


def local(
    tokens,
    lengths,
    kv_cache,
    w_qkv,
    w_headgate,
    w_out,
    in_gain,
    q_gain,
    k_gain,
    post_gain,
    w_gate,
    w_up,
    w_down,
    final_gain,
    w_vocab,
):
    rows, width = tokens.shape
    head_dim = q_gain.shape[1]
    columns = w_qkv.shape[3]
    units = w_gate.shape[2]
    seg = width // (X * C)
    part_width = width // C
    req = lax.axis_index(("y", "z"))
    ix, ic = lax.axis_index("x"), lax.axis_index("c")

    sent, ffn, normed = first(tokens, in_gain, w_out[0].T, w_gate[0].T, w_up[0].T, w_down[0])
    ffn = lax.all_gather(ffn, ("y", "x"), axis=0).reshape(Y, X, -1, seg)
    qkv_block = lax.all_gather(w_qkv[0, :, 0], "y", axis=0, tiled=True)

    positions = lax.dynamic_slice_in_dim(lengths, req * rows, rows)
    starts = jnp.cumsum(positions) - positions
    limits = starts + positions

    head_gate = jax.nn.sigmoid(jnp.dot(normed, w_headgate[0], preferred_element_type=F32))

    half = head_dim // 2
    frequency = ROPE_THETA ** (-2.0 * jnp.arange(half, dtype=F32) / head_dim)
    angles = positions.astype(F32)[:, None] * frequency[None, :]
    cosine, sine = jnp.cos(angles), jnp.sin(angles)

    def own_row(array):
        return lax.dynamic_slice_in_dim(array, ix, 1, 0)

    def own_core(array, axis):
        return lax.dynamic_slice_in_dim(array, ic, 1, axis)

    residual = own_core(own_row(tokens).reshape(Y, C, seg), 1).reshape(8, head_dim)
    slot = jnp.arange(kv_cache.shape[2], dtype=jnp.int32)
    inside = (slot[None, :] >= starts[:, None]) & (slot[None, :] < limits[:, None])
    inside = inside.astype(F32)

    depth = width // (Y * Z)
    arrived, post_gain = lax.optimization_barrier((swap(sent, "z"), post_gain))
    post_half = own_core(post_gain.reshape(X, C, seg), 1).reshape(X, seg)
    batch = arrived[:, :rows].reshape(Z * rows, Y * depth)
    out_block = arrived[:, 8:].reshape(Z, 2, -1, head_dim).transpose(1, 0, 2, 3).reshape(2, -1, head_dim)
    part = jnp.dot(batch, qkv_block, preferred_element_type=F32).astype(BF16)
    part = swap(part.reshape(Z, rows, columns), "z")
    part, out_block, head_gate, cosine, sine, residual, post_half, inside = lax.optimization_barrier(
        (part, out_block, head_gate, cosine, sine, residual, post_half, inside)
    )
    qkv = jnp.sum(part.astype(F32), axis=0)

    query = qkv[:, : 2 * head_dim].reshape(rows, 2, head_dim)
    query = rotate(rms_scale(query, q_gain[0]), cosine[:, None], sine[:, None]).astype(BF16)
    key = qkv[:, 2 * head_dim : 3 * head_dim]
    key = rotate(rms_scale(key, k_gain[0]), cosine, sine).astype(BF16)
    value = qkv[:, 3 * head_dim :].astype(BF16)

    scale = head_dim ** (-0.5)
    keys, values = kv_cache[0, 0, :, 0], kv_cache[0, 1, :, 0]
    score = jnp.einsum("rqd,sd->rqs", query, keys, preferred_element_type=F32) * scale
    weight = jnp.where(inside[:, None, :] > 0.0, jnp.exp(score), 0.0)
    own = jnp.exp(jnp.sum(query.astype(F32) * key.astype(F32)[:, None], axis=-1) * scale)
    total = jnp.sum(weight, axis=-1) + own
    summed = jnp.einsum("rqs,sd->rqd", weight.astype(BF16), values, preferred_element_type=F32)
    summed = summed + own.astype(BF16).astype(F32)[..., None] * value.astype(F32)[:, None]
    attended = summed / total[..., None]
    mixed = (attended * head_gate[..., None]).astype(BF16)

    everyone = spread(mixed.transpose(1, 0, 2).reshape(2 * rows, head_dim), "y", Y).reshape(Y, 2, rows, head_dim)
    part = jnp.einsum("yqrd,qnd->yrn", everyone, out_block, preferred_element_type=F32)
    part = swap(part.reshape(Y * rows * C, 2, head_dim), ("y", "x", "c"))
    projected = jnp.sum(part.reshape(Y, X * C, 2, head_dim), axis=1).reshape(8, head_dim)
    stream = (residual.astype(F32) + projected).astype(BF16)

    gate_up = ffn[:, :, : 2 * units].transpose(0, 2, 1, 3).reshape(Y * 2 * units, part_width)
    down = ffn[:, :, 2 * units :].transpose(0, 2, 1, 3).reshape(Y * units, part_width)
    batch, gate_up, down = lax.optimization_barrier((spread(stream, "z", Z), gate_up, down))
    batch = batch.reshape(Z, X, seg)
    wide = batch.astype(F32)
    squares = jnp.sum(wide * wide, axis=(1, 2)).reshape(Z, 1)
    batch = (wide * post_half).astype(BF16).reshape(Z, part_width)
    part = lax.dot_general(batch, gate_up, (((1,), (1,)), ((), ())), preferred_element_type=F32)
    part = jnp.concatenate([part, jnp.broadcast_to(squares, (Z, head_dim))], axis=1)
    both = jnp.sum(lax.all_gather(part, "c", axis=0), axis=0)
    scale = lax.rsqrt(both[:, -1:] / width + EPSILON)
    both = (both[:, :-head_dim] * scale).reshape(Z, Y, 2 * units)
    hidden = (jax.nn.silu(both[..., :units]) * both[..., units:]).astype(BF16)
    part = jnp.dot(hidden.reshape(Z, Y * units), down, preferred_element_type=F32).astype(BF16)
    lowered = jnp.sum(swap(part.reshape(Z, 8, head_dim), "z").astype(F32), axis=0)
    piece = (stream.astype(F32) + lowered).astype(BF16)

    piece = spread(piece, "z", Z).reshape(Z, part_width)
    near = spread(piece, ("y", "x"), Y * X).reshape(Y * X * Z, part_width)
    far = lax.ppermute(near, "c", [(0, 1), (1, 0)])
    near, far = near.astype(F32), far.astype(F32)
    mean_square = (jnp.sum(near * near, axis=-1, keepdims=True) + jnp.sum(far * far, axis=-1, keepdims=True)) / width
    scale = lax.rsqrt(mean_square + EPSILON)

    def scored(half, core):
        gain = lax.dynamic_slice_in_dim(final_gain.reshape(X, C, seg), core, 1, 1).reshape(1, part_width)
        vocab = lax.dynamic_slice_in_dim(w_vocab.reshape(X, C, seg, -1), core, 1, 1).reshape(part_width, -1)
        return jnp.dot((half * scale * gain).astype(BF16), vocab, preferred_element_type=F32)

    logits = (scored(near, ic) + scored(far, 1 - ic)).astype(BF16)
    logits = logits.reshape(Y, X, Z, w_vocab.shape[1]).transpose(0, 2, 1, 3)
    return logits.reshape(Y * X * Z, w_vocab.shape[1])


def solution(mesh):
    fine = Mesh(mesh.devices.reshape(Y, Z, X, C), ("y", "z", "x", "c"))
    req, head = ("y", "z"), ("x", "c")
    in_specs = (
        P(req, None),
        P(),
        P(None, None, req, head, None),
        P(None, req, head, None),
        P(None, None, head),
        P(None, head, req),
        P(),
        P(),
        P(),
        P(),
        P(None, head, req),
        P(None, head, req),
        P(None, req, head),
        P(),
        P(None, req + head),
    )
    out_specs = P(None, req + head)
    return jax.shard_map(local, mesh=fine, in_specs=in_specs, out_specs=out_specs, check_vma=False)
```

```python
import jax
import jax.numpy as jnp
from jax import lax
from jax.sharding import Mesh
from jax.sharding import PartitionSpec as P

EPSILON = 1e-06
ROPE_THETA = 1000000.0
Y, Z, X, C = 4, 16, 4, 2
ZH, ZL = 4, 4
DEPTH = ("zh", "zl")
F32, BF16 = jnp.float32, jnp.bfloat16


def rms_scale(values, gain):
    mean_square = jnp.mean(values * values, axis=-1, keepdims=True)
    return values * lax.rsqrt(mean_square + EPSILON) * gain


def rotate(values, cosine, sine):
    half = values.shape[-1] // 2
    a, b = values[..., :half], values[..., half:]
    return jnp.concatenate([a * cosine - b * sine, b * cosine + a * sine], axis=-1)


def swap(values, axes):
    return lax.all_to_all(values, axes, split_axis=0, concat_axis=0, tiled=True)


def spread(values, axes, count):
    return swap(jnp.broadcast_to(values[None], (count,) + values.shape), axes)


def local(
    tokens,
    lengths,
    kv_cache,
    w_qkv,
    w_headgate,
    w_out,
    in_gain,
    q_gain,
    k_gain,
    post_gain,
    w_gate,
    w_up,
    w_down,
    final_gain,
    w_vocab,
):
    rows, width = tokens.shape
    head_dim = q_gain.shape[1]
    columns = w_qkv.shape[3]
    units = w_gate.shape[2]
    seg = width // (X * C)
    part_width = width // C
    req = lax.axis_index(("y",) + DEPTH)
    ix, ic = lax.axis_index("x"), lax.axis_index("c")

    ffn = jnp.concatenate([w_gate[0].T, w_up[0].T, w_down[0]], axis=0)
    ffn = lax.all_gather(ffn, ("y", "x"), axis=0).reshape(Y, X, -1, seg)
    qkv_block = lax.all_gather(w_qkv[0, :, 0], "y", axis=0, tiled=True)

    positions = lax.dynamic_slice_in_dim(lengths, req * rows, rows)
    starts = jnp.cumsum(positions) - positions
    limits = starts + positions

    token_wide = tokens.astype(F32)
    gained = (token_wide * in_gain[0]).astype(BF16)
    in_scale = lax.rsqrt(jnp.mean(token_wide * token_wide, axis=-1, keepdims=True) + EPSILON)
    normed = (token_wide * in_scale * in_gain[0]).astype(BF16)
    head_gate = jax.nn.sigmoid(jnp.dot(normed, w_headgate[0], preferred_element_type=F32))

    half = head_dim // 2
    frequency = ROPE_THETA ** (-2.0 * jnp.arange(half, dtype=F32) / head_dim)
    angles = positions.astype(F32)[:, None] * frequency[None, :]
    cosine, sine = jnp.cos(angles), jnp.sin(angles)

    def own_row(array):
        return lax.dynamic_slice_in_dim(array, ix, 1, 0)

    def own_core(array, axis):
        return lax.dynamic_slice_in_dim(array, ic, 1, axis)

    residual = own_core(own_row(tokens).reshape(Y, C, seg), 1).reshape(8, head_dim)
    slot = jnp.arange(kv_cache.shape[2], dtype=jnp.int32)
    inside = (slot[None, :] >= starts[:, None]) & (slot[None, :] < limits[:, None])
    inside = inside.astype(F32)

    depth = width // (Y * Z)
    sent = gained.reshape(rows, Y, Z, depth).transpose(2, 0, 1, 3).reshape(Z, rows, Y * depth)
    block = w_out[0].T
    block = jnp.concatenate([block[:, :head_dim], block[:, head_dim:]], axis=0)
    sent = jnp.concatenate(
        [sent, jnp.zeros((Z, 8 - rows, head_dim), BF16), jnp.broadcast_to(block[None], (Z,) + block.shape)], axis=1
    )
    arrived = swap(sent, DEPTH)
    arrived, qkv_block, post_gain = lax.optimization_barrier((arrived, qkv_block, post_gain))
    post_half = own_core(post_gain.reshape(X, C, seg), 1).reshape(X, seg)
    batch = arrived[:, :rows].reshape(Z * rows, Y * depth)
    out_block = arrived[:, 8:].reshape(Z, 2, -1, head_dim).transpose(1, 0, 2, 3).reshape(2, -1, head_dim)
    part = jnp.dot(batch, qkv_block, preferred_element_type=F32).astype(BF16)
    part = swap(part.reshape(Z, rows, columns), DEPTH)
    part, out_block, in_scale, head_gate, cosine, sine, residual, post_half, inside = lax.optimization_barrier(
        (part, out_block, in_scale, head_gate, cosine, sine, residual, post_half, inside)
    )
    qkv = jnp.sum(part.astype(F32), axis=0) * in_scale

    query = qkv[:, : 2 * head_dim].reshape(rows, 2, head_dim)
    query = rotate(rms_scale(query, q_gain[0]), cosine[:, None], sine[:, None]).astype(BF16)
    key = qkv[:, 2 * head_dim : 3 * head_dim]
    key = rotate(rms_scale(key, k_gain[0]), cosine, sine).astype(BF16)
    value = qkv[:, 3 * head_dim :].astype(BF16)

    scale = head_dim ** (-0.5)
    keys, values = kv_cache[0, 0, :, 0], kv_cache[0, 1, :, 0]
    score = jnp.einsum("rqd,sd->rqs", query, keys, preferred_element_type=F32) * scale
    weight = jnp.where(inside[:, None, :] > 0.0, jnp.exp(score), 0.0)
    own = jnp.exp(jnp.sum(query.astype(F32) * key.astype(F32)[:, None], axis=-1) * scale)
    total = jnp.sum(weight, axis=-1) + own
    summed = jnp.einsum("rqs,sd->rqd", weight.astype(BF16), values, preferred_element_type=F32)
    summed = summed + own.astype(BF16).astype(F32)[..., None] * value.astype(F32)[:, None]
    attended = summed / total[..., None]
    mixed = (attended * head_gate[..., None]).astype(BF16)

    everyone = spread(mixed.transpose(1, 0, 2).reshape(2 * rows, head_dim), "y", Y).reshape(Y, 2, rows, head_dim)
    part = jnp.einsum("yqrd,qnd->yrn", everyone, out_block, preferred_element_type=F32)
    part = swap(part.reshape(Y * rows * C, 2, head_dim), ("y", "x", "c"))
    projected = jnp.sum(part.reshape(Y, X * C, 2, head_dim), axis=1).reshape(8, head_dim)
    stream = (residual.astype(F32) + projected).astype(BF16)

    batch = spread(stream, DEPTH, Z).reshape(Z, X, seg)
    wide = batch.astype(F32)
    squares = jnp.sum(wide * wide, axis=(1, 2)).reshape(Z, 1)
    batch = (wide * post_half).astype(BF16)
    part = jnp.einsum("bxk,yxfk->byf", batch, ffn[:, :, : 2 * units], preferred_element_type=F32)
    part = jnp.concatenate([part.reshape(Z, -1), jnp.broadcast_to(squares, (Z, head_dim))], axis=1)
    both = jnp.sum(lax.all_gather(part, "c", axis=0), axis=0)
    scale = lax.rsqrt(both[:, -1:] / width + EPSILON)
    both = (both[:, :-head_dim] * scale).reshape(Z, Y, 2 * units)
    hidden = (jax.nn.silu(both[..., :units]) * both[..., units:]).astype(BF16)
    down = ffn[:, :, 2 * units : 3 * units]
    part = jnp.einsum("byf,yxfk->bxk", hidden, down, preferred_element_type=F32).astype(BF16)
    part = jnp.sum(spread(part.reshape(Z, 8, head_dim), "zh", ZH).astype(F32), axis=0).astype(BF16)
    lowered = jnp.sum(spread(part, "zl", ZL).astype(F32), axis=0)
    piece = (wide.reshape(Z, 8, head_dim) + lowered).astype(BF16).reshape(Z, part_width)

    near = spread(piece, ("y", "x"), Y * X).reshape(Y * X * Z, part_width)
    far = lax.ppermute(near, "c", [(0, 1), (1, 0)])
    near, far = near.astype(F32), far.astype(F32)
    mean_square = (jnp.sum(near * near, axis=-1, keepdims=True) + jnp.sum(far * far, axis=-1, keepdims=True)) / width
    scale = lax.rsqrt(mean_square + EPSILON)

    def scored(half, core):
        gain = lax.dynamic_slice_in_dim(final_gain.reshape(X, C, seg), core, 1, 1).reshape(1, part_width)
        vocab = lax.dynamic_slice_in_dim(w_vocab.reshape(X, C, seg, -1), core, 1, 1).reshape(part_width, -1)
        return jnp.dot((half * scale * gain).astype(BF16), vocab, preferred_element_type=F32)

    logits = (scored(near, ic) + scored(far, 1 - ic)).astype(BF16)
    logits = logits.reshape(Y, X, Z, w_vocab.shape[1]).transpose(0, 2, 1, 3)
    return logits.reshape(Y * X * Z, w_vocab.shape[1])


def solution(mesh):
    fine = Mesh(mesh.devices.reshape(Y, ZH, ZL, X, C), ("y", "zh", "zl", "x", "c"))
    req, head = ("y",) + DEPTH, ("x", "c")
    in_specs = (
        P(req, None),
        P(),
        P(None, None, req, head, None),
        P(None, req, head, None),
        P(None, None, head),
        P(None, head, req),
        P(),
        P(),
        P(),
        P(),
        P(None, head, req),
        P(None, head, req),
        P(None, req, head),
        P(),
        P(None, req + head),
    )
    out_specs = P(None, req + head)
    return jax.shard_map(local, mesh=fine, in_specs=in_specs, out_specs=out_specs, check_vma=False)
```

```python
import jax
import jax.numpy as jnp
from jax import lax
from jax.sharding import Mesh
from jax.sharding import PartitionSpec as P

EPSILON = 1e-06
ROPE_THETA = 1000000.0
Y, Z, X, C = 4, 16, 4, 2
ZH, ZL = 4, 4
DEPTH = ("zh", "zl")
F32, BF16 = jnp.float32, jnp.bfloat16


def rms_scale(values, gain):
    mean_square = jnp.mean(values * values, axis=-1, keepdims=True)
    return values * lax.rsqrt(mean_square + EPSILON) * gain


def rotate(values, cosine, sine):
    half = values.shape[-1] // 2
    a, b = values[..., :half], values[..., half:]
    return jnp.concatenate([a * cosine - b * sine, b * cosine + a * sine], axis=-1)


def swap(values, axes):
    return lax.all_to_all(values, axes, split_axis=0, concat_axis=0, tiled=True)


def spread(values, axes, count):
    return swap(jnp.broadcast_to(values[None], (count,) + values.shape), axes)


def local(
    tokens,
    lengths,
    kv_cache,
    w_qkv,
    w_headgate,
    w_out,
    in_gain,
    q_gain,
    k_gain,
    post_gain,
    w_gate,
    w_up,
    w_down,
    final_gain,
    w_vocab,
):
    rows, width = tokens.shape
    head_dim = q_gain.shape[1]
    columns = w_qkv.shape[3]
    units = w_gate.shape[2]
    seg = width // (X * C)
    part_width = width // C
    req = lax.axis_index(("y",) + DEPTH)
    ix, ic = lax.axis_index("x"), lax.axis_index("c")

    ffn = jnp.concatenate([w_gate[0].T, w_up[0].T, w_down[0]], axis=0)
    ffn = lax.all_gather(ffn, ("y", "x"), axis=0).reshape(Y, X, -1, seg)
    qkv_block = lax.all_gather(w_qkv[0, :, 0], "y", axis=0, tiled=True)

    positions = lax.dynamic_slice_in_dim(lengths, req * rows, rows)
    starts = jnp.cumsum(positions) - positions
    limits = starts + positions

    token_wide = tokens.astype(F32)
    gained = (token_wide * in_gain[0]).astype(BF16)
    in_scale = lax.rsqrt(jnp.mean(token_wide * token_wide, axis=-1, keepdims=True) + EPSILON)
    normed = (token_wide * in_scale * in_gain[0]).astype(BF16)
    head_gate = jax.nn.sigmoid(jnp.dot(normed, w_headgate[0], preferred_element_type=F32))

    half = head_dim // 2
    frequency = ROPE_THETA ** (-2.0 * jnp.arange(half, dtype=F32) / head_dim)
    angles = positions.astype(F32)[:, None] * frequency[None, :]
    cosine, sine = jnp.cos(angles), jnp.sin(angles)

    def own_row(array):
        return lax.dynamic_slice_in_dim(array, ix, 1, 0)

    def own_core(array, axis):
        return lax.dynamic_slice_in_dim(array, ic, 1, axis)

    residual = own_core(own_row(tokens).reshape(Y, C, seg), 1).reshape(8, head_dim)
    slot = jnp.arange(kv_cache.shape[2], dtype=jnp.int32)
    inside = (slot[None, :] >= starts[:, None]) & (slot[None, :] < limits[:, None])
    inside = inside.astype(F32)

    depth = width // (Y * Z)
    sent = gained.reshape(rows, Y, Z, depth).transpose(2, 0, 1, 3).reshape(Z, rows, Y * depth)
    block = w_out[0].T
    block = jnp.concatenate([block[:, :head_dim], block[:, head_dim:]], axis=0)
    sent = jnp.concatenate(
        [sent, jnp.zeros((Z, 8 - rows, head_dim), BF16), jnp.broadcast_to(block[None], (Z,) + block.shape)], axis=1
    )
    arrived = swap(sent, DEPTH)
    arrived, qkv_block, post_gain = lax.optimization_barrier((arrived, qkv_block, post_gain))
    post_half = own_core(post_gain.reshape(X, C, seg), 1).reshape(X, seg)
    batch = arrived[:, :rows].reshape(Z * rows, Y * depth)
    out_block = arrived[:, 8:].reshape(Z, 2, -1, head_dim).transpose(1, 0, 2, 3).reshape(2, -1, head_dim)
    part = jnp.dot(batch, qkv_block, preferred_element_type=F32).astype(BF16)
    part = swap(part.reshape(Z, rows, columns), DEPTH)
    part, out_block, in_scale, head_gate, cosine, sine, residual, post_half, inside = lax.optimization_barrier(
        (part, out_block, in_scale, head_gate, cosine, sine, residual, post_half, inside)
    )
    qkv = jnp.sum(part.astype(F32), axis=0) * in_scale

    query = qkv[:, : 2 * head_dim].reshape(rows, 2, head_dim)
    query = rotate(rms_scale(query, q_gain[0]), cosine[:, None], sine[:, None]).astype(BF16)
    key = qkv[:, 2 * head_dim : 3 * head_dim]
    key = rotate(rms_scale(key, k_gain[0]), cosine, sine).astype(BF16)
    value = qkv[:, 3 * head_dim :].astype(BF16)

    scale = head_dim ** (-0.5)
    keys, values = kv_cache[0, 0, :, 0], kv_cache[0, 1, :, 0]
    score = jnp.einsum("rqd,sd->rqs", query, keys, preferred_element_type=F32) * scale
    weight = jnp.where(inside[:, None, :] > 0.0, jnp.exp(score), 0.0)
    own = jnp.exp(jnp.sum(query.astype(F32) * key.astype(F32)[:, None], axis=-1) * scale)
    total = jnp.sum(weight, axis=-1) + own
    summed = jnp.einsum("rqs,sd->rqd", weight.astype(BF16), values, preferred_element_type=F32)
    summed = summed + own.astype(BF16).astype(F32)[..., None] * value.astype(F32)[:, None]
    attended = summed / total[..., None]
    mixed = (attended * head_gate[..., None]).astype(BF16)

    everyone = spread(mixed.transpose(1, 0, 2).reshape(2 * rows, head_dim), "y", Y).reshape(Y, 2, rows, head_dim)
    part = jnp.einsum("yqrd,qnd->yrn", everyone, out_block, preferred_element_type=F32)
    part = swap(part.reshape(Y * rows * C, 2, head_dim), ("y", "x", "c"))
    projected = jnp.sum(part.reshape(Y, X * C, 2, head_dim), axis=1).reshape(8, head_dim)
    stream = (residual.astype(F32) + projected).astype(BF16)

    gate_up = ffn[:, :, : 2 * units].transpose(1, 0, 2, 3)
    down = ffn[:, :, 2 * units :]
    batch, gate_up, down = lax.optimization_barrier((spread(stream, DEPTH, Z), gate_up, down))
    batch = batch.reshape(Z, X, seg)
    wide = batch.astype(F32)
    squares = jnp.sum(wide * wide, axis=(1, 2)).reshape(Z, 1)
    batch = (wide * post_half).astype(BF16)
    part = jnp.einsum("bxk,xyfk->byf", batch, gate_up, preferred_element_type=F32)
    part = jnp.concatenate([part.reshape(Z, -1), jnp.broadcast_to(squares, (Z, head_dim))], axis=1)
    both = jnp.sum(lax.all_gather(part, "c", axis=0), axis=0)
    scale = lax.rsqrt(both[:, -1:] / width + EPSILON)
    both = (both[:, :-head_dim] * scale).reshape(Z, Y, 2 * units)
    hidden = (jax.nn.silu(both[..., :units]) * both[..., units:]).astype(BF16)
    part = jnp.einsum("byf,yxfk->bxk", hidden, down, preferred_element_type=F32).astype(BF16)
    part = jnp.sum(spread(part.reshape(Z, 8, head_dim), "zh", ZH).astype(F32), axis=0).astype(BF16)
    lowered = jnp.sum(spread(part, "zl", ZL).astype(F32), axis=0)
    piece = (wide.reshape(Z, 8, head_dim) + lowered).astype(BF16).reshape(Z, part_width)

    near = spread(piece, ("y", "x"), Y * X).reshape(Y * X * Z, part_width)
    far = lax.ppermute(near, "c", [(0, 1), (1, 0)])
    near, far = near.astype(F32), far.astype(F32)
    mean_square = (jnp.sum(near * near, axis=-1, keepdims=True) + jnp.sum(far * far, axis=-1, keepdims=True)) / width
    scale = lax.rsqrt(mean_square + EPSILON)

    def scored(half, core):
        gain = lax.dynamic_slice_in_dim(final_gain.reshape(X, C, seg), core, 1, 1).reshape(1, part_width)
        vocab = lax.dynamic_slice_in_dim(w_vocab.reshape(X, C, seg, -1), core, 1, 1).reshape(part_width, -1)
        return jnp.dot((half * scale * gain).astype(BF16), vocab, preferred_element_type=F32)

    logits = (scored(near, ic) + scored(far, 1 - ic)).astype(BF16)
    logits = logits.reshape(Y, X, Z, w_vocab.shape[1]).transpose(0, 2, 1, 3)
    return logits.reshape(Y * X * Z, w_vocab.shape[1])


def solution(mesh):
    fine = Mesh(mesh.devices.reshape(Y, ZH, ZL, X, C), ("y", "zh", "zl", "x", "c"))
    req, head = ("y",) + DEPTH, ("x", "c")
    in_specs = (
        P(req, None),
        P(),
        P(None, None, req, head, None),
        P(None, req, head, None),
        P(None, None, head),
        P(None, head, req),
        P(),
        P(),
        P(),
        P(),
        P(None, head, req),
        P(None, head, req),
        P(None, req, head),
        P(),
        P(None, req + head),
    )
    out_specs = P(None, req + head)
    return jax.shard_map(local, mesh=fine, in_specs=in_specs, out_specs=out_specs, check_vma=False)
```

```python
import jax
import jax.numpy as jnp
from jax import lax
from jax.sharding import Mesh
from jax.sharding import PartitionSpec as P

EPSILON = 1e-06
ROPE_THETA = 1000000.0
Y, Z, X, C = 4, 16, 4, 2
ZH, ZL = 4, 4
DEPTH = ("zh", "zl")
F32, BF16 = jnp.float32, jnp.bfloat16


def rms_scale(values, gain):
    mean_square = jnp.mean(values * values, axis=-1, keepdims=True)
    return values * lax.rsqrt(mean_square + EPSILON) * gain


def rotate(values, cosine, sine):
    half = values.shape[-1] // 2
    a, b = values[..., :half], values[..., half:]
    return jnp.concatenate([a * cosine - b * sine, b * cosine + a * sine], axis=-1)


def swap(values, axes):
    return lax.all_to_all(values, axes, split_axis=0, concat_axis=0, tiled=True)


def spread(values, axes, count):
    return swap(jnp.broadcast_to(values[None], (count,) + values.shape), axes)


def local(
    tokens,
    lengths,
    kv_cache,
    w_qkv,
    w_headgate,
    w_out,
    in_gain,
    q_gain,
    k_gain,
    post_gain,
    w_gate,
    w_up,
    w_down,
    final_gain,
    w_vocab,
):
    rows, width = tokens.shape
    head_dim = q_gain.shape[1]
    columns = w_qkv.shape[3]
    units = w_gate.shape[2]
    seg = width // (X * C)
    part_width = width // C
    req = lax.axis_index(("y",) + DEPTH)
    ix, ic = lax.axis_index("x"), lax.axis_index("c")

    ffn = jnp.concatenate([w_gate[0].T, w_up[0].T, w_down[0]], axis=0)
    ffn = lax.all_gather(ffn, ("y", "x"), axis=0).reshape(Y, X, -1, seg)
    qkv_block = lax.all_gather(w_qkv[0, :, 0], "y", axis=0, tiled=True)

    positions = lax.dynamic_slice_in_dim(lengths, req * rows, rows)
    starts = jnp.cumsum(positions) - positions
    limits = starts + positions

    token_wide = tokens.astype(F32)
    gained = (token_wide * in_gain[0]).astype(BF16)
    in_scale = lax.rsqrt(jnp.mean(token_wide * token_wide, axis=-1, keepdims=True) + EPSILON)
    normed = (token_wide * in_scale * in_gain[0]).astype(BF16)
    head_gate = jax.nn.sigmoid(jnp.dot(normed, w_headgate[0], preferred_element_type=F32))

    half = head_dim // 2
    frequency = ROPE_THETA ** (-2.0 * jnp.arange(half, dtype=F32) / head_dim)
    angles = positions.astype(F32)[:, None] * frequency[None, :]
    cosine, sine = jnp.cos(angles), jnp.sin(angles)

    def own_row(array):
        return lax.dynamic_slice_in_dim(array, ix, 1, 0)

    def own_core(array, axis):
        return lax.dynamic_slice_in_dim(array, ic, 1, axis)

    residual = own_core(own_row(tokens).reshape(Y, C, seg), 1).reshape(8, head_dim)
    slot = jnp.arange(kv_cache.shape[2], dtype=jnp.int32)
    inside = (slot[None, :] >= starts[:, None]) & (slot[None, :] < limits[:, None])

    depth = width // (Y * Z)
    sent = gained.reshape(rows, Y, Z, depth).transpose(2, 0, 1, 3).reshape(Z, rows, Y * depth)
    block = w_out[0].T
    halves = [jnp.broadcast_to(block[None, :, q * head_dim : (q + 1) * head_dim], (Z, block.shape[0], head_dim)) for q in (0, 1)]
    sent = jnp.concatenate([sent, jnp.zeros((Z, 8 - rows, head_dim), BF16)] + halves, axis=1)
    arrived = swap(sent, DEPTH)
    arrived, qkv_block, in_scale, head_gate, cosine, sine, residual, inside = lax.optimization_barrier(
        (arrived, qkv_block, in_scale, head_gate, cosine, sine, residual, inside)
    )
    batch = arrived[:, :rows].reshape(Z * rows, Y * depth)
    out_block = arrived[:, 8:].reshape(Z, 2, -1, head_dim).transpose(1, 0, 2, 3).reshape(2, -1, head_dim)
    part = jnp.dot(batch, qkv_block, preferred_element_type=F32).astype(BF16)
    part, out_block = lax.optimization_barrier((part.reshape(Z, rows, columns), out_block))
    part = swap(part, DEPTH)
    qkv = jnp.sum(part.astype(F32), axis=0) * in_scale

    query = qkv[:, : 2 * head_dim].reshape(rows, 2, head_dim)
    query = rotate(rms_scale(query, q_gain[0]), cosine[:, None], sine[:, None]).astype(BF16)
    key = qkv[:, 2 * head_dim : 3 * head_dim]
    key = rotate(rms_scale(key, k_gain[0]), cosine, sine).astype(BF16)
    value = qkv[:, 3 * head_dim :].astype(BF16)

    scale = head_dim ** (-0.5)
    keys, values = kv_cache[0, 0, :, 0], kv_cache[0, 1, :, 0]
    score = jnp.einsum("rqd,sd->rqs", query, keys, preferred_element_type=F32) * scale
    weight = jnp.where(inside[:, None, :], jnp.exp(score), 0.0)
    own = jnp.exp(jnp.sum(query.astype(F32) * key.astype(F32)[:, None], axis=-1) * scale)
    total = jnp.sum(weight, axis=-1) + own
    summed = jnp.einsum("rqs,sd->rqd", weight.astype(BF16), values, preferred_element_type=F32)
    summed = summed + own.astype(BF16).astype(F32)[..., None] * value.astype(F32)[:, None]
    attended = summed / total[..., None]
    mixed = (attended * head_gate[..., None]).astype(BF16)

    everyone = spread(mixed.transpose(1, 0, 2).reshape(2 * rows, head_dim), "y", Y).reshape(Y, 2, rows, head_dim)
    part = jnp.einsum("yqrd,qnd->yrn", everyone, out_block, preferred_element_type=F32)
    part = swap(part.reshape(Y * rows * C, 2, head_dim), ("y", "x", "c"))
    projected = jnp.sum(part.reshape(Y, X * C, 2, head_dim), axis=1).reshape(8, head_dim)
    stream = (residual.astype(F32) + projected).astype(BF16)

    stream, post_gain = lax.optimization_barrier((stream, post_gain))
    post_half = own_core(post_gain.reshape(X, C, seg), 1).reshape(X, seg)
    gate_up = ffn[:, :, : 2 * units].transpose(1, 0, 2, 3)
    down = ffn[:, :, 2 * units :]
    batch, gate_up, down, post_half = lax.optimization_barrier((spread(stream, DEPTH, Z), gate_up, down, post_half))
    batch = batch.reshape(Z, X, seg)
    wide = batch.astype(F32)
    squares = jnp.sum(wide * wide, axis=(1, 2)).reshape(Z, 1)
    batch = (wide * post_half).astype(BF16)
    part = jnp.einsum("bxk,xyfk->byf", batch, gate_up, preferred_element_type=F32)
    part = jnp.concatenate([part.reshape(Z, -1), jnp.broadcast_to(squares, (Z, head_dim))], axis=1)
    both = jnp.sum(lax.all_gather(part, "c", axis=0), axis=0)
    scale = lax.rsqrt(both[:, -1:] / width + EPSILON)
    both = (both[:, :-head_dim] * scale).reshape(Z, Y, 2 * units)
    hidden = (jax.nn.silu(both[..., :units]) * both[..., units:]).astype(BF16)
    part = jnp.einsum("byf,yxfk->bxk", hidden, down, preferred_element_type=F32).astype(BF16)
    part = jnp.sum(spread(part.reshape(Z, 8, head_dim), "zh", ZH).astype(F32), axis=0).astype(BF16)
    lowered = jnp.sum(spread(part, "zl", ZL).astype(F32), axis=0)
    piece = (wide.reshape(Z, 8, head_dim) + lowered).astype(BF16).reshape(Z, part_width)

    near = spread(piece, ("y", "x"), Y * X).reshape(Y * X * Z, part_width)
    far = lax.ppermute(near, "c", [(0, 1), (1, 0)])
    near, far = near.astype(F32), far.astype(F32)
    mean_square = (jnp.sum(near * near, axis=-1, keepdims=True) + jnp.sum(far * far, axis=-1, keepdims=True)) / width
    scale = lax.rsqrt(mean_square + EPSILON)

    def scored(half, core):
        gain = lax.dynamic_slice_in_dim(final_gain.reshape(X, C, seg), core, 1, 1).reshape(1, part_width)
        vocab = lax.dynamic_slice_in_dim(w_vocab.reshape(X, C, seg, -1), core, 1, 1).reshape(part_width, -1)
        return jnp.dot((half * scale * gain).astype(BF16), vocab, preferred_element_type=F32)

    logits = (scored(near, ic) + scored(far, 1 - ic)).astype(BF16)
    logits = logits.reshape(Y, X, Z, w_vocab.shape[1]).transpose(0, 2, 1, 3)
    return logits.reshape(Y * X * Z, w_vocab.shape[1])


def solution(mesh):
    fine = Mesh(mesh.devices.reshape(Y, ZH, ZL, X, C), ("y", "zh", "zl", "x", "c"))
    req, head = ("y",) + DEPTH, ("x", "c")
    in_specs = (
        P(req, None),
        P(),
        P(None, None, req, head, None),
        P(None, req, head, None),
        P(None, None, head),
        P(None, head, req),
        P(),
        P(),
        P(),
        P(),
        P(None, head, req),
        P(None, head, req),
        P(None, req, head),
        P(),
        P(None, req + head),
    )
    out_specs = P(None, req + head)
    return jax.shard_map(local, mesh=fine, in_specs=in_specs, out_specs=out_specs, check_vma=False)
```

```python
import jax
import jax.numpy as jnp
from jax import lax
from jax.sharding import Mesh
from jax.sharding import PartitionSpec as P

EPSILON = 1e-06
ROPE_THETA = 1000000.0
Y, Z, X, C = 4, 16, 4, 2
ZH, ZL = 4, 4
DEPTH = ("zh", "zl")
F32, BF16 = jnp.float32, jnp.bfloat16


def rms_scale(values, gain):
    mean_square = jnp.mean(values * values, axis=-1, keepdims=True)
    return values * lax.rsqrt(mean_square + EPSILON) * gain


def rotate(values, cosine, sine):
    half = values.shape[-1] // 2
    a, b = values[..., :half], values[..., half:]
    return jnp.concatenate([a * cosine - b * sine, b * cosine + a * sine], axis=-1)


def swap(values, axes):
    return lax.all_to_all(values, axes, split_axis=0, concat_axis=0, tiled=True)


def spread(values, axes, count):
    return swap(jnp.broadcast_to(values[None], (count,) + values.shape), axes)


def local(
    tokens,
    lengths,
    kv_cache,
    w_qkv,
    w_headgate,
    w_out,
    in_gain,
    q_gain,
    k_gain,
    post_gain,
    w_gate,
    w_up,
    w_down,
    final_gain,
    w_vocab,
):
    rows, width = tokens.shape
    head_dim = q_gain.shape[1]
    columns = w_qkv.shape[3]
    units = w_gate.shape[2]
    seg = width // (X * C)
    part_width = width // C
    req = lax.axis_index(("y",) + DEPTH)
    ix, ic = lax.axis_index("x"), lax.axis_index("c")

    ffn = jnp.concatenate([w_gate[0].T, w_up[0].T, w_down[0]], axis=0)
    ffn = lax.all_gather(ffn, ("y", "x"), axis=0).reshape(Y, X, -1, seg)
    qkv_block = lax.all_gather(w_qkv[0, :, 0], "y", axis=0, tiled=True)

    positions = lax.dynamic_slice_in_dim(lengths, req * rows, rows)
    starts = jnp.cumsum(positions) - positions
    limits = starts + positions

    token_wide = tokens.astype(F32)
    gained = (token_wide * in_gain[0]).astype(BF16)
    in_scale = lax.rsqrt(jnp.mean(token_wide * token_wide, axis=-1, keepdims=True) + EPSILON)
    normed = (token_wide * in_scale * in_gain[0]).astype(BF16)
    head_gate = jax.nn.sigmoid(jnp.dot(normed, w_headgate[0], preferred_element_type=F32))

    half = head_dim // 2
    frequency = ROPE_THETA ** (-2.0 * jnp.arange(half, dtype=F32) / head_dim)
    angles = positions.astype(F32)[:, None] * frequency[None, :]
    cosine, sine = jnp.cos(angles), jnp.sin(angles)

    def own_row(array):
        return lax.dynamic_slice_in_dim(array, ix, 1, 0)

    def own_core(array, axis):
        return lax.dynamic_slice_in_dim(array, ic, 1, axis)

    residual = own_core(own_row(tokens).reshape(Y, C, seg), 1).reshape(8, head_dim)
    slot = jnp.arange(kv_cache.shape[2], dtype=jnp.int32)
    inside = (slot[None, :] >= starts[:, None]) & (slot[None, :] < limits[:, None])

    depth = width // (Y * Z)
    sent = gained.reshape(rows, Y, Z, depth).transpose(2, 0, 1, 3).reshape(Z, rows, Y * depth)
    block = w_out[0].T
    halves = [jnp.broadcast_to(block[None, :, q * head_dim : (q + 1) * head_dim], (Z, block.shape[0], head_dim)) for q in (0, 1)]
    sent = jnp.concatenate([sent, jnp.zeros((Z, 8 - rows, head_dim), BF16)] + halves, axis=1)
    arrived = swap(sent, DEPTH)
    arrived, qkv_block, in_scale, head_gate, cosine, sine, residual, inside = lax.optimization_barrier(
        (arrived, qkv_block, in_scale, head_gate, cosine, sine, residual, inside)
    )
    batch = arrived[:, :rows].reshape(Z * rows, Y * depth)
    out_block = arrived[:, 8:].reshape(Z, 2, -1, head_dim).transpose(1, 0, 2, 3).reshape(2, -1, head_dim)
    part = jnp.dot(batch, qkv_block, preferred_element_type=F32).astype(BF16)
    part, out_block = lax.optimization_barrier((part.reshape(Z, rows, columns), out_block))
    part = swap(part, DEPTH)
    qkv = jnp.sum(part.astype(F32), axis=0) * in_scale

    query = qkv[:, : 2 * head_dim].reshape(rows, 2, head_dim)
    query = rotate(rms_scale(query, q_gain[0]), cosine[:, None], sine[:, None]).astype(BF16)
    key = qkv[:, 2 * head_dim : 3 * head_dim]
    key = rotate(rms_scale(key, k_gain[0]), cosine, sine).astype(BF16)
    value = qkv[:, 3 * head_dim :].astype(BF16)

    scale = head_dim ** (-0.5)
    keys, values = kv_cache[0, 0, :, 0], kv_cache[0, 1, :, 0]
    score = jnp.einsum("rqd,sd->rqs", query, keys, preferred_element_type=F32) * scale
    weight = jnp.where(inside[:, None, :], jnp.exp(score), 0.0)
    own = jnp.exp(jnp.sum(query.astype(F32) * key.astype(F32)[:, None], axis=-1) * scale)
    total = jnp.sum(weight, axis=-1) + own
    summed = jnp.einsum("rqs,sd->rqd", weight.astype(BF16), values, preferred_element_type=F32)
    summed = summed + own.astype(BF16).astype(F32)[..., None] * value.astype(F32)[:, None]
    attended = summed / total[..., None]
    mixed = (attended * head_gate[..., None]).astype(BF16)

    everyone = spread(mixed.transpose(1, 0, 2).reshape(2 * rows, head_dim), "y", Y).reshape(Y, 2, rows, head_dim)
    part = jnp.einsum("yqrd,qnd->yrn", everyone, out_block, preferred_element_type=F32)
    part = swap(part.reshape(Y * rows * C, 2, head_dim), ("y", "x", "c"))
    projected = jnp.sum(part.reshape(Y, X * C, 2, head_dim), axis=1).reshape(8, head_dim)
    stream = (residual.astype(F32) + projected).astype(BF16)

    stream, post_gain = lax.optimization_barrier((stream, post_gain))
    post_half = own_core(post_gain.reshape(X, C, seg), 1).reshape(X, seg)
    gate_up = ffn[:, :, : 2 * units].transpose(1, 0, 2, 3)
    down = ffn[:, :, 2 * units :]
    batch, gate_up, down, post_half = lax.optimization_barrier((spread(stream, DEPTH, Z), gate_up, down, post_half))
    batch = batch.reshape(Z, X, seg)
    wide = batch.astype(F32)
    squares = jnp.sum(wide * wide, axis=(1, 2)).reshape(Z, 1)
    batch = (wide * post_half).astype(BF16)
    part = jnp.einsum("bxk,xyfk->byf", batch, gate_up, preferred_element_type=F32)
    part = jnp.concatenate([part.reshape(Z, -1), jnp.broadcast_to(squares, (Z, head_dim))], axis=1)
    both = jnp.sum(lax.all_gather(part, "c", axis=0), axis=0)
    scale = lax.rsqrt(both[:, -1:] / width + EPSILON)
    both = (both[:, :-head_dim] * scale).reshape(Z, Y, 2 * units)
    hidden = (jax.nn.silu(both[..., :units]) * both[..., units:]).astype(BF16)
    part = jnp.einsum("byf,yxfk->bxk", hidden, down, preferred_element_type=F32).astype(BF16)
    part = jnp.sum(spread(part.reshape(Z, 8, head_dim), "zl", ZL).astype(F32), axis=0).astype(BF16)
    lowered = jnp.sum(spread(part, "zh", ZH).astype(F32), axis=0)
    piece = (wide.reshape(Z, 8, head_dim) + lowered).astype(BF16).reshape(Z, part_width)

    near = spread(piece, ("y", "x"), Y * X).reshape(Y * X * Z, part_width)
    far = lax.ppermute(near, "c", [(0, 1), (1, 0)])
    near, far = near.astype(F32), far.astype(F32)
    mean_square = (jnp.sum(near * near, axis=-1, keepdims=True) + jnp.sum(far * far, axis=-1, keepdims=True)) / width
    scale = lax.rsqrt(mean_square + EPSILON)

    def scored(half, core):
        gain = lax.dynamic_slice_in_dim(final_gain.reshape(X, C, seg), core, 1, 1).reshape(1, part_width)
        vocab = lax.dynamic_slice_in_dim(w_vocab.reshape(X, C, seg, -1), core, 1, 1).reshape(part_width, -1)
        return jnp.dot((half * scale * gain).astype(BF16), vocab, preferred_element_type=F32)

    logits = (scored(near, ic) + scored(far, 1 - ic)).astype(BF16)
    logits = logits.reshape(Y, X, Z, w_vocab.shape[1]).transpose(0, 2, 1, 3)
    return logits.reshape(Y * X * Z, w_vocab.shape[1])


def solution(mesh):
    fine = Mesh(mesh.devices.reshape(Y, ZH, ZL, X, C), ("y", "zh", "zl", "x", "c"))
    req, head = ("y",) + DEPTH, ("x", "c")
    in_specs = (
        P(req, None),
        P(),
        P(None, None, req, head, None),
        P(None, req, head, None),
        P(None, None, head),
        P(None, head, req),
        P(),
        P(),
        P(),
        P(),
        P(None, head, req),
        P(None, head, req),
        P(None, req, head),
        P(),
        P(None, req + head),
    )
    out_specs = P(None, req + head)
    return jax.shard_map(local, mesh=fine, in_specs=in_specs, out_specs=out_specs, check_vma=False)
```

```python
import jax
import jax.numpy as jnp
from jax import lax
from jax.sharding import Mesh
from jax.sharding import PartitionSpec as P

EPSILON = 1e-06
ROPE_THETA = 1000000.0
Y, Z, X, C = 4, 16, 4, 2
ZH, ZL = 4, 4
DEPTH = ("zh", "zl")
F32, BF16 = jnp.float32, jnp.bfloat16


def rms_scale(values, gain):
    mean_square = jnp.mean(values * values, axis=-1, keepdims=True)
    return values * lax.rsqrt(mean_square + EPSILON) * gain


def rotate(values, cosine, sine):
    half = values.shape[-1] // 2
    a, b = values[..., :half], values[..., half:]
    return jnp.concatenate([a * cosine - b * sine, b * cosine + a * sine], axis=-1)


def swap(values, axes):
    return lax.all_to_all(values, axes, split_axis=0, concat_axis=0, tiled=True)


def spread(values, axes, count):
    return swap(jnp.broadcast_to(values[None], (count,) + values.shape), axes)


def local(
    tokens,
    lengths,
    kv_cache,
    w_qkv,
    w_headgate,
    w_out,
    in_gain,
    q_gain,
    k_gain,
    post_gain,
    w_gate,
    w_up,
    w_down,
    final_gain,
    w_vocab,
):
    rows, width = tokens.shape
    head_dim = q_gain.shape[1]
    columns = w_qkv.shape[3]
    units = w_gate.shape[2]
    seg = width // (X * C)
    part_width = width // C
    req = lax.axis_index(("y",) + DEPTH)
    ix, ic = lax.axis_index("x"), lax.axis_index("c")

    ffn = jnp.concatenate([w_gate[0].T, w_up[0].T, w_down[0]], axis=0)
    qkv_block = lax.all_gather(w_qkv[0, :, 0], "y", axis=0, tiled=True)

    positions = lax.dynamic_slice_in_dim(lengths, req * rows, rows)
    starts = jnp.cumsum(positions) - positions
    limits = starts + positions

    token_wide = tokens.astype(F32)
    gained = (token_wide * in_gain[0]).astype(BF16)
    in_scale = lax.rsqrt(jnp.mean(token_wide * token_wide, axis=-1, keepdims=True) + EPSILON)
    normed = (token_wide * in_scale * in_gain[0]).astype(BF16)
    head_gate = jax.nn.sigmoid(jnp.dot(normed, w_headgate[0], preferred_element_type=F32))

    half = head_dim // 2
    frequency = ROPE_THETA ** (-2.0 * jnp.arange(half, dtype=F32) / head_dim)
    angles = positions.astype(F32)[:, None] * frequency[None, :]
    cosine, sine = jnp.cos(angles), jnp.sin(angles)

    def own_row(array):
        return lax.dynamic_slice_in_dim(array, ix, 1, 0)

    def own_core(array, axis):
        return lax.dynamic_slice_in_dim(array, ic, 1, axis)

    residual = own_core(own_row(tokens).reshape(Y, C, seg), 1).reshape(8, head_dim)
    slot = jnp.arange(kv_cache.shape[2], dtype=jnp.int32)
    inside = (slot[None, :] >= starts[:, None]) & (slot[None, :] < limits[:, None])

    depth = width // (Y * Z)
    sent = gained.reshape(rows, Y, Z, depth).transpose(2, 0, 1, 3).reshape(Z, rows, Y * depth)
    block = w_out[0].T
    halves = [jnp.broadcast_to(block[None, :, q * head_dim : (q + 1) * head_dim], (Z, block.shape[0], head_dim)) for q in (0, 1)]
    sent = jnp.concatenate([sent, jnp.zeros((Z, 8 - rows, head_dim), BF16)] + halves, axis=1)
    arrived = swap(sent, DEPTH)
    arrived, qkv_block, in_scale, head_gate, cosine, sine, residual, inside, ffn = lax.optimization_barrier(
        (arrived, qkv_block, in_scale, head_gate, cosine, sine, residual, inside, ffn)
    )
    ffn = lax.all_gather(ffn, "x", axis=0)
    batch = arrived[:, :rows].reshape(Z * rows, Y * depth)
    out_block = arrived[:, 8:].reshape(Z, 2, -1, head_dim).transpose(1, 0, 2, 3).reshape(2, -1, head_dim)
    part = jnp.dot(batch, qkv_block, preferred_element_type=F32).astype(BF16)
    part, out_block = lax.optimization_barrier((part.reshape(Z, rows, columns), out_block))
    part, ffn = lax.optimization_barrier((swap(part, DEPTH), ffn))
    qkv = jnp.sum(part.astype(F32), axis=0) * in_scale

    query = qkv[:, : 2 * head_dim].reshape(rows, 2, head_dim)
    query = rotate(rms_scale(query, q_gain[0]), cosine[:, None], sine[:, None]).astype(BF16)
    key = qkv[:, 2 * head_dim : 3 * head_dim]
    key = rotate(rms_scale(key, k_gain[0]), cosine, sine).astype(BF16)
    value = qkv[:, 3 * head_dim :].astype(BF16)

    scale = head_dim ** (-0.5)
    keys, values = kv_cache[0, 0, :, 0], kv_cache[0, 1, :, 0]
    score = jnp.einsum("rqd,sd->rqs", query, keys, preferred_element_type=F32) * scale
    weight = jnp.where(inside[:, None, :], jnp.exp(score), 0.0)
    own = jnp.exp(jnp.sum(query.astype(F32) * key.astype(F32)[:, None], axis=-1) * scale)
    total = jnp.sum(weight, axis=-1) + own
    summed = jnp.einsum("rqs,sd->rqd", weight.astype(BF16), values, preferred_element_type=F32)
    summed = summed + own.astype(BF16).astype(F32)[..., None] * value.astype(F32)[:, None]
    attended = summed / total[..., None]
    mixed = (attended * head_gate[..., None]).astype(BF16)

    sent = jnp.broadcast_to(mixed.transpose(1, 0, 2).reshape(1, 2 * rows, head_dim), (Y, 2 * rows, head_dim))
    residual = residual.reshape(Y, 2, head_dim)
    arrived = swap(jnp.concatenate([sent, residual, jnp.zeros((Y, 6, head_dim), BF16)], axis=1), "y")
    everyone = arrived[:, : 2 * rows].reshape(Y, 2, rows, head_dim)
    residual = arrived[:, 2 * rows : 2 * rows + 2].reshape(8, head_dim)
    part = jnp.einsum("yqrd,qnd->yrn", everyone, out_block, preferred_element_type=F32)
    part = part.reshape(Y, rows, C, seg).transpose(1, 2, 0, 3).reshape(rows * C, 8, head_dim)
    projected = jnp.sum(swap(part, ("x", "c")), axis=0)
    stream = (residual.astype(F32) + projected).astype(BF16)

    post_half = own_core(post_gain.reshape(X, C, seg), 1).reshape(X, seg)
    batch = spread(stream, ("y",) + DEPTH, Y * Z).reshape(Y, Z, Y, seg)
    batch = batch.transpose(2, 1, 0, 3).reshape(Y * Z, X, seg)
    wide = batch.astype(F32)
    squares = jnp.sum(wide * wide, axis=(1, 2)).reshape(Y * Z, 1)
    gained = (wide * post_half).astype(BF16)
    part = jnp.einsum("bxk,xfk->bf", gained, ffn[:, : 2 * units], preferred_element_type=F32)
    part = jnp.concatenate([part, jnp.broadcast_to(squares, (Y * Z, 64))], axis=1)
    both = jnp.sum(lax.all_gather(part, "c", axis=0), axis=0)
    scale = lax.rsqrt(both[:, -1:] / width + EPSILON)
    both = both[:, : 2 * units] * scale
    hidden = (jax.nn.silu(both[:, :units]) * both[:, units:]).astype(BF16)
    part = jnp.einsum("bf,xfk->bxk", hidden, ffn[:, 2 * units :], preferred_element_type=F32).astype(BF16)
    part = jnp.sum(swap(part.reshape(Y, Z, 8, head_dim), "y").astype(F32), axis=0).astype(BF16)
    wide = lax.dynamic_slice_in_dim(batch.reshape(Y, Z, X * seg), lax.axis_index("y"), 1, 0).astype(F32)
    part = jnp.sum(spread(part.reshape(Z, 8, head_dim), "zl", ZL).astype(F32), axis=0).astype(BF16)
    lowered = jnp.sum(spread(part, "zh", ZH).astype(F32), axis=0)
    piece = (wide.reshape(Z, 8, head_dim) + lowered).astype(BF16).reshape(Z, part_width)

    near = spread(piece, ("y", "x"), Y * X).reshape(Y * X * Z, part_width)
    far = lax.ppermute(near, "c", [(0, 1), (1, 0)])
    near, far = near.astype(F32), far.astype(F32)
    mean_square = (jnp.sum(near * near, axis=-1, keepdims=True) + jnp.sum(far * far, axis=-1, keepdims=True)) / width
    scale = lax.rsqrt(mean_square + EPSILON)

    def scored(half, core):
        gain = lax.dynamic_slice_in_dim(final_gain.reshape(X, C, seg), core, 1, 1).reshape(1, part_width)
        vocab = lax.dynamic_slice_in_dim(w_vocab.reshape(X, C, seg, -1), core, 1, 1).reshape(part_width, -1)
        return jnp.dot((half * scale * gain).astype(BF16), vocab, preferred_element_type=F32)

    logits = (scored(near, ic) + scored(far, 1 - ic)).astype(BF16)
    logits = logits.reshape(Y, X, Z, w_vocab.shape[1]).transpose(0, 2, 1, 3)
    return logits.reshape(Y * X * Z, w_vocab.shape[1])


def solution(mesh):
    fine = Mesh(mesh.devices.reshape(Y, ZH, ZL, X, C), ("y", "zh", "zl", "x", "c"))
    req, head = ("y",) + DEPTH, ("x", "c")
    in_specs = (
        P(req, None),
        P(),
        P(None, None, req, head, None),
        P(None, req, head, None),
        P(None, None, head),
        P(None, head, req),
        P(),
        P(),
        P(),
        P(),
        P(None, head, req),
        P(None, head, req),
        P(None, req, head),
        P(),
        P(None, req + head),
    )
    out_specs = P(None, req + head)
    return jax.shard_map(local, mesh=fine, in_specs=in_specs, out_specs=out_specs, check_vma=False)
```

```python
import jax
import jax.numpy as jnp
from jax import lax
from jax.sharding import Mesh
from jax.sharding import PartitionSpec as P

EPSILON = 1e-06
ROPE_THETA = 1000000.0
Y, Z, X, C = 4, 16, 4, 2
ZH, ZL = 4, 4
DEPTH = ("zh", "zl")
F32, BF16 = jnp.float32, jnp.bfloat16


def rms_scale(values, gain):
    mean_square = jnp.mean(values * values, axis=-1, keepdims=True)
    return values * lax.rsqrt(mean_square + EPSILON) * gain


def rotate(values, cosine, sine):
    half = values.shape[-1] // 2
    a, b = values[..., :half], values[..., half:]
    return jnp.concatenate([a * cosine - b * sine, b * cosine + a * sine], axis=-1)


def swap(values, axes):
    return lax.all_to_all(values, axes, split_axis=0, concat_axis=0, tiled=True)


def spread(values, axes, count):
    return swap(jnp.broadcast_to(values[None], (count,) + values.shape), axes)


def local(
    tokens,
    lengths,
    kv_cache,
    w_qkv,
    w_headgate,
    w_out,
    in_gain,
    q_gain,
    k_gain,
    post_gain,
    w_gate,
    w_up,
    w_down,
    final_gain,
    w_vocab,
):
    rows, width = tokens.shape
    head_dim = q_gain.shape[1]
    columns = w_qkv.shape[3]
    units = w_gate.shape[2]
    seg = width // (X * C)
    part_width = width // C
    req = lax.axis_index(("y",) + DEPTH)
    ix, ic = lax.axis_index("x"), lax.axis_index("c")

    ffn = jnp.concatenate([w_gate[0].T, w_up[0].T, w_down[0]], axis=0)
    ffn = lax.all_gather(ffn, ("y", "x"), axis=0).reshape(Y, X, -1, seg)
    qkv_block = lax.all_gather(w_qkv[0, :, 0], "y", axis=0, tiled=True)

    positions = lax.dynamic_slice_in_dim(lengths, req * rows, rows)
    starts = jnp.cumsum(positions) - positions
    limits = starts + positions

    token_wide = tokens.astype(F32)
    gained = (token_wide * in_gain[0]).astype(BF16)
    in_scale = lax.rsqrt(jnp.mean(token_wide * token_wide, axis=-1, keepdims=True) + EPSILON)
    normed = (token_wide * in_scale * in_gain[0]).astype(BF16)
    head_gate = jax.nn.sigmoid(jnp.dot(normed, w_headgate[0], preferred_element_type=F32))

    half = head_dim // 2
    frequency = ROPE_THETA ** (-2.0 * jnp.arange(half, dtype=F32) / head_dim)
    angles = positions.astype(F32)[:, None] * frequency[None, :]
    cosine, sine = jnp.cos(angles), jnp.sin(angles)

    def own_row(array):
        return lax.dynamic_slice_in_dim(array, ix, 1, 0)

    def own_core(array, axis):
        return lax.dynamic_slice_in_dim(array, ic, 1, axis)

    residual = own_core(own_row(tokens).reshape(Y, C, seg), 1).reshape(Y, 2, head_dim)
    residual = jnp.concatenate([residual, jnp.zeros((Y, 6, head_dim), BF16)], axis=1)
    slot = jnp.arange(kv_cache.shape[2], dtype=jnp.int32)
    inside = (slot[None, :] >= starts[:, None]) & (slot[None, :] < limits[:, None])

    depth = width // (Y * Z)
    sent = gained.reshape(rows, Y, Z, depth).transpose(2, 0, 1, 3).reshape(Z, rows, Y * depth)
    block = w_out[0].T
    halves = [jnp.broadcast_to(block[None, :, q * head_dim : (q + 1) * head_dim], (Z, block.shape[0], head_dim)) for q in (0, 1)]
    sent = jnp.concatenate([sent, jnp.zeros((Z, 8 - rows, head_dim), BF16)] + halves, axis=1)
    arrived = swap(sent, DEPTH)
    arrived, qkv_block, in_scale, head_gate, cosine, sine, residual, inside = lax.optimization_barrier(
        (arrived, qkv_block, in_scale, head_gate, cosine, sine, residual, inside)
    )
    batch = arrived[:, :rows].reshape(Z * rows, Y * depth)
    out_block = arrived[:, 8:].reshape(Z, 2, -1, head_dim).transpose(1, 0, 2, 3).reshape(2, -1, head_dim)
    part = jnp.dot(batch, qkv_block, preferred_element_type=F32).astype(BF16)
    part, out_block = lax.optimization_barrier((part.reshape(Z, rows, columns), out_block))
    part = swap(part, DEPTH)
    qkv = jnp.sum(part.astype(F32), axis=0) * in_scale

    query = qkv[:, : 2 * head_dim].reshape(rows, 2, head_dim)
    query = rotate(rms_scale(query, q_gain[0]), cosine[:, None], sine[:, None]).astype(BF16)
    key = qkv[:, 2 * head_dim : 3 * head_dim]
    key = rotate(rms_scale(key, k_gain[0]), cosine, sine).astype(BF16)
    value = qkv[:, 3 * head_dim :].astype(BF16)

    scale = head_dim ** (-0.5)
    keys, values = kv_cache[0, 0, :, 0], kv_cache[0, 1, :, 0]
    score = jnp.einsum("rqd,sd->rqs", query, keys, preferred_element_type=F32) * scale
    weight = jnp.where(inside[:, None, :], jnp.exp(score), 0.0)
    own = jnp.exp(jnp.sum(query.astype(F32) * key.astype(F32)[:, None], axis=-1) * scale)
    total = jnp.sum(weight, axis=-1) + own
    summed = jnp.einsum("rqs,sd->rqd", weight.astype(BF16), values, preferred_element_type=F32)
    summed = summed + own.astype(BF16).astype(F32)[..., None] * value.astype(F32)[:, None]
    attended = summed / total[..., None]
    mixed = (attended * head_gate[..., None]).astype(BF16)

    sent = jnp.broadcast_to(mixed.transpose(1, 0, 2).reshape(1, 2 * rows, head_dim), (Y, 2 * rows, head_dim))
    arrived = swap(jnp.concatenate([sent, residual], axis=1), "y")
    everyone = arrived[:, : 2 * rows].reshape(Y, 2, rows, head_dim)
    residual = arrived[:, 2 * rows : 2 * rows + 2].reshape(8, head_dim)
    part = jnp.einsum("yqrd,qnd->yrn", everyone, out_block, preferred_element_type=F32)
    part = part.reshape(Y, rows, C, seg).transpose(1, 2, 0, 3).reshape(rows * C, 8, head_dim)
    part, residual = lax.optimization_barrier((part, residual))
    projected = jnp.sum(swap(part, ("x", "c")), axis=0)
    stream = (residual.astype(F32) + projected).astype(BF16)

    stream, post_gain = lax.optimization_barrier((stream, post_gain))
    post_half = own_core(post_gain.reshape(X, C, seg), 1).reshape(X, seg)
    gate_up = ffn[:, :, : 2 * units].transpose(1, 0, 2, 3)
    down = ffn[:, :, 2 * units :]
    sent = jnp.broadcast_to(stream.reshape(Y, 1, 2, head_dim), (Y, Z, 2, head_dim)).reshape(Y * Z, 2, head_dim)
    batch, gate_up, down, post_half = lax.optimization_barrier((swap(sent, ("y",) + DEPTH), gate_up, down, post_half))
    batch = batch.reshape(Y, Z, seg).transpose(1, 0, 2)
    wide = batch.astype(F32)
    squares = jnp.sum(wide * wide, axis=(1, 2)).reshape(Z, 1)
    batch = (wide * post_half).astype(BF16)
    part = jnp.einsum("bxk,xyfk->byf", batch, gate_up, preferred_element_type=F32)
    part = jnp.concatenate([part.reshape(Z, -1), jnp.broadcast_to(squares, (Z, head_dim))], axis=1)
    both = jnp.sum(lax.all_gather(part, "c", axis=0), axis=0)
    scale = lax.rsqrt(both[:, -1:] / width + EPSILON)
    both = (both[:, :-head_dim] * scale).reshape(Z, Y, 2 * units)
    hidden = (jax.nn.silu(both[..., :units]) * both[..., units:]).astype(BF16)
    part = jnp.einsum("byf,yxfk->bxk", hidden, down, preferred_element_type=F32).astype(BF16)
    part, wide = lax.optimization_barrier((part, wide.reshape(Z, 8, head_dim)))
    part = jnp.sum(spread(part.reshape(Z, 8, head_dim), "zl", ZL).astype(F32), axis=0).astype(BF16)
    lowered = jnp.sum(spread(part, "zh", ZH).astype(F32), axis=0)
    piece = (wide + lowered).astype(BF16).reshape(Z, part_width)

    near = spread(piece, ("y", "x"), Y * X).reshape(Y * X * Z, part_width)
    far = lax.ppermute(near, "c", [(0, 1), (1, 0)])
    near, far = near.astype(F32), far.astype(F32)
    mean_square = (jnp.sum(near * near, axis=-1, keepdims=True) + jnp.sum(far * far, axis=-1, keepdims=True)) / width
    scale = lax.rsqrt(mean_square + EPSILON)

    def scored(half, core):
        gain = lax.dynamic_slice_in_dim(final_gain.reshape(X, C, seg), core, 1, 1).reshape(1, part_width)
        vocab = lax.dynamic_slice_in_dim(w_vocab.reshape(X, C, seg, -1), core, 1, 1).reshape(part_width, -1)
        return jnp.dot((half * scale * gain).astype(BF16), vocab, preferred_element_type=F32)

    logits = (scored(near, ic) + scored(far, 1 - ic)).astype(BF16)
    logits = logits.reshape(Y, X, Z, w_vocab.shape[1]).transpose(0, 2, 1, 3)
    return logits.reshape(Y * X * Z, w_vocab.shape[1])


def solution(mesh):
    fine = Mesh(mesh.devices.reshape(Y, ZH, ZL, X, C), ("y", "zh", "zl", "x", "c"))
    req, head = ("y",) + DEPTH, ("x", "c")
    in_specs = (
        P(req, None),
        P(),
        P(None, None, req, head, None),
        P(None, req, head, None),
        P(None, None, head),
        P(None, head, req),
        P(),
        P(),
        P(),
        P(),
        P(None, head, req),
        P(None, head, req),
        P(None, req, head),
        P(),
        P(None, req + head),
    )
    out_specs = P(None, req + head)
    return jax.shard_map(local, mesh=fine, in_specs=in_specs, out_specs=out_specs, check_vma=False)
```
